128 devices in a mesh: shard: 4 (over z_hi, core), rep: 32 (over y, x, z_lo).
Axes of the slice: x: 4, y: 4, z: 4 (z_hi: 2, z_lo: 2; z = z_hi * 2 + z_lo), core: 2. Of those that a mesh axis runs over, the one named last changes fastest.
Arguments:
- tokens: bfloat16 [49152, 4608], P(('shard', 'rep')), may hold values from -6 to 6
- norm_gain: float32 [4608], replicated, may hold values from 0.25 to 1.75
- key_grad: bfloat16 [49152, 1024], P(('shard', 'rep')), may hold values from -6 to 6
- key_weight: bfloat16 [4608, 1024], P('shard'), may hold values from -0.09375 to 0.09375
- m_code: bfloat16 [4608, 1024], P('shard'), may hold values from -127 to 127, as said below
- m_exp: int32 [4608, 4], P('shard'), may hold values from 3 to 7
- v_code: bfloat16 [4608, 1024], P('shard'), may hold values from 1 to 255, as said below
- v_exp: int32 [4608, 4], P('shard'), may hold values from 4 to 9
Outputs:
- keys: bfloat16 [49152, 1024], P(('shard', 'rep'))
- token_grad: bfloat16 [49152, 4608], P(('shard', 'rep'))
- adam_step: float32 [4608, 1024], P('shard')
- m_rel: bfloat16 [4608, 1024], P('shard')
- m_scale: float32 [4608, 4], P('shard')
- v_rel: bfloat16 [4608, 1024], P('shard')
- v_scale: float32 [4608, 4], P('shard')
The draws below stay inside these ranges and needn't reach their ends.
Inputs may be any that keep to these rules, and one draw needn't show every extreme that they name: `m_code`: whole numbers. `v_code`: whole numbers.
All inputs are finite; a program needn't handle non-finite values. Where the reference program divides by a largest or mean magnitude, that divisor is 1e-20 or more.
Results may differ from the reference program's by a relative error of at most 0.0099.
Values may be sent and summed in bfloat16 or wider, within the bound.
No kernel may reach another device: no remote copies, remote signals or barrier semaphores. Data moves between devices by JAX's collectives and lax.ppermute only.
A program may use at most 192 MiB of HBM per device.

```python
import jax
import jax.numpy as jnp
from jax import lax

D = 4608
KH = 1024
NB = 4
TOKENS = 49152


def draw_m_code(key, part):
    return jax.random.randint(key, (D, KH), -127, 128).astype(jnp.float32).astype(jnp.bfloat16)


def draw_v_code(key, part):
    return jax.random.randint(key, (D, KH), 1, 256).astype(jnp.float32).astype(jnp.bfloat16)


def place_ends(values, stream_key, smallest, largest):
    extent = values.shape
    index_at = [jax.random.randint(jax.random.fold_in(stream_key, axis), (), 0, extent[axis]) for axis in range(len(extent))]
    values = values.at[tuple(index_at)].set(smallest)
    longest = extent.index(max(extent))
    index_at[longest] = (index_at[longest] + 1) % extent[longest]
    return values.at[tuple(index_at)].set(largest)


def steps_of(own_key, dims, shards, smallest, largest):
    def one(dim, parts):
        steps = jax.random.uniform(jax.random.fold_in(jax.random.fold_in(own_key, 6), dim), (parts,), jnp.float32, smallest / len(shards), largest / len(shards))
        return jnp.repeat(jnp.exp(steps), dims[dim] // parts).reshape((-1,) + (1,) * (len(dims) - dim - 1))

    level = one(*shards[0])
    for cut in shards[1:]:
        level = level * one(*cut)
    return level


def bell_draw(stream_key, dims, scale, most, split=(), kind=jnp.bfloat16):
    drawn = scale * jax.random.normal(stream_key, dims, jnp.float32)
    if split:
        drawn = drawn * steps_of(stream_key, dims, split, -0.22, 0.18)
    return jnp.clip(drawn, -most, most).astype(kind)


def setup_inputs(seed: int = 0) -> dict:
    streams_of = jax.random.split(jax.random.key(seed), 9)
    return {
        "tokens": bell_draw(streams_of[0], (TOKENS, D), 1.0, 6.0, ((0, 128),)),
        "norm_gain": jnp.clip(1.0 + 0.15 * jax.random.normal(streams_of[1], (D,), jnp.float32), 0.25, 1.75),
        "key_grad": bell_draw(streams_of[2], (TOKENS, KH), 1.0, 6.0, ((0, 128),)),
        "key_weight": bell_draw(streams_of[3], (D, KH), D ** -0.5, 0.09375, ((0, 4),)),
        "m_code": draw_m_code(jax.random.fold_in(streams_of[8], 71), 0),
        "m_exp": place_ends(jax.random.randint(streams_of[5], (D, NB), 3, 8), jax.random.fold_in(streams_of[5], 1), 3, 7).astype(jnp.int32),
        "v_code": draw_v_code(jax.random.fold_in(streams_of[8], 71), 0),
        "v_exp": place_ends(jax.random.randint(streams_of[7], (D, NB), 4, 10), jax.random.fold_in(streams_of[7], 1), 4, 9).astype(jnp.int32),
    }


bias_first = 0.9999734386011124
bias_second = 0.0952078528862904

def requantize(grad, m_code, m_exp, v_code, v_exp):
    rows, width = grad.shape
    blocks = m_exp.shape[1]
    size = width // blocks
    g3 = grad.reshape(rows, blocks, size)
    m_old = m_code.astype(jnp.float32).reshape(rows, blocks, size) * (jnp.exp2(m_exp.astype(jnp.float32)) / 127.0)[:, :, None]
    v_old = v_code.astype(jnp.float32).reshape(rows, blocks, size) * (jnp.exp2(v_exp.astype(jnp.float32)) / 255.0)[:, :, None]
    m_new = 0.9 * m_old + 0.1 * g3
    v_new = 0.999 * v_old + 0.001 * g3 * g3
    step = m_new / bias_first / (jnp.sqrt(v_new / bias_second) + 1e-08)
    m_scale = lax.optimization_barrier(jnp.max(jnp.abs(m_new), axis=2))
    v_scale = lax.optimization_barrier(jnp.max(v_new, axis=2))
    m_rel = (m_new / (m_scale + 1e-06)[:, :, None]).reshape(rows, width).astype(jnp.bfloat16)
    v_rel = (v_new / (v_scale + 1e-06)[:, :, None]).reshape(rows, width).astype(jnp.bfloat16)
    return (step.reshape(rows, width), m_rel, m_scale, v_rel, v_scale)

def reference(tokens, norm_gain, key_grad, key_weight, m_code, m_exp, v_code, v_exp):
    x = tokens.astype(jnp.float32)
    inv = lax.rsqrt(lax.optimization_barrier(jnp.mean(x * x, axis=1, keepdims=True)) + 1e-06)
    normed = (x * inv * norm_gain).astype(jnp.bfloat16)
    keys = jnp.dot(normed, key_weight, preferred_element_type=jnp.float32).astype(jnp.bfloat16)
    dnormed = lax.dot_general(key_grad, key_weight, (((1,), (1,)), ((), ())), preferred_element_type=jnp.float32)
    scaled = dnormed * norm_gain
    inner = lax.optimization_barrier(jnp.mean(scaled * x, axis=1, keepdims=True))
    token_grad = (inv * scaled - x * inv * inv * inv * inner).astype(jnp.bfloat16)
    grad = lax.dot_general(normed, key_grad, (((0,), (0,)), ((), ())), preferred_element_type=jnp.float32)
    step, m_rel, m_scale, v_rel, v_scale = requantize(grad, m_code, m_exp, v_code, v_exp)
    return (keys, token_grad, step, m_rel, m_scale, v_rel, v_scale)
```

```python
import jax
import jax.numpy as jnp
from jax import lax
from jax.experimental import pallas as pl
from jax.experimental.pallas import tpu as pltpu
from jax.sharding import Mesh, PartitionSpec as P

bias_first = 0.9999734386011124
bias_second = 0.0952078528862904

AXES = ("zh", "c", "y", "x", "zl")
CHIPS = ("zh", "y", "x", "zl")
REPLICAS = ("y", "x", "zl")

D = 4608
KH = 1024
ROWS = 1152
T = 384
RB, CB = 144, 256


def index_of(zh, c, y, x, zl):
    return (((zh * 2 + c) * 4 + y) * 4 + x) * 2 + zl


def pairs(move):
    out = []
    for zh in range(2):
        for c in range(2):
            for y in range(4):
                for x in range(4):
                    for zl in range(2):
                        to = move(zh, c, y, x, zl)
                        out.append((index_of(zh, c, y, x, zl), index_of(*to)))
    return out


def partner(zh, c, y, x, zl):
    return zh, 1 - c, y, x, zl


def across(zh, c, y, x, zl):
    return 1 - zh, c, y, x, 1 - zl


def around(step):
    def move(zh, c, y, x, zl):
        if c == 0:
            return zh, c, y, (x + step) % 4, zl
        return zh, c, (y + step) % 4, x, zl

    return move


def send(value, move):
    return lax.ppermute(value, AXES, pairs(move))


def norm_kernel(core, x_ref, gain_ref, mine_ref, theirs_ref, inv_ref):
    x = x_ref[...].astype(jnp.float32)
    inv = lax.rsqrt(jnp.mean(x * x, axis=1, keepdims=True) + 1e-06)
    inv_ref[...] = inv
    c = core[0]
    for half in range(2):
        for out, which in ((mine_ref, c), (theirs_ref, 1 - c)):
            cols = pl.ds(pl.multiple_of(half * 2 * ROWS + which * ROWS, 128), ROWS)
            part = x_ref[:, cols].astype(jnp.float32) * inv * gain_ref[:, cols]
            out[:, half * ROWS:(half + 1) * ROWS] = part.astype(jnp.bfloat16)


def norm_call(core, tokens, gain):
    tm = 128
    return pl.pallas_call(
        norm_kernel,
        grid_spec=pltpu.PrefetchScalarGridSpec(
            num_scalar_prefetch=1,
            grid=(T // tm,),
            in_specs=[
                pl.BlockSpec((tm, D), lambda i, core: (i, 0)),
                pl.BlockSpec((1, D), lambda i, core: (0, 0)),
            ],
            out_specs=[
                pl.BlockSpec((tm, D // 2), lambda i, core: (i, 0)),
                pl.BlockSpec((tm, D // 2), lambda i, core: (i, 0)),
                pl.BlockSpec((tm, 1), lambda i, core: (i, 0)),
            ],
        ),
        out_shape=[
            jax.ShapeDtypeStruct((T, D // 2), jnp.bfloat16),
            jax.ShapeDtypeStruct((T, D // 2), jnp.bfloat16),
            jax.ShapeDtypeStruct((T, 1), jnp.float32),
        ],
        cost_estimate=pl.CostEstimate(flops=6 * T * D, bytes_accessed=4 * T * D, transcendentals=T),
        name="norm",
    )(core, tokens, gain)


def grad_kernel(a_ref, b_ref, ka_ref, kb_ref, out_ref):
    dims = (((0,), (0,)), ((), ()))
    acc = lax.dot_general(a_ref[...], ka_ref[...], dims, preferred_element_type=jnp.float32)
    acc += lax.dot_general(b_ref[...], kb_ref[...], dims, preferred_element_type=jnp.float32)
    for rb in range(8):
        for cb in range(4):
            piece = acc[rb * RB:(rb + 1) * RB, cb * CB:(cb + 1) * CB]
            out_ref[rb * 4 + cb] = piece.astype(jnp.bfloat16)


def grad_call(a, b, ka, kb):
    return pl.pallas_call(
        grad_kernel,
        grid=(2,),
        in_specs=[
            pl.BlockSpec((T, ROWS), lambda i: (0, i)),
            pl.BlockSpec((T, ROWS), lambda i: (0, i)),
            pl.BlockSpec((T, KH), lambda i: (0, 0)),
            pl.BlockSpec((T, KH), lambda i: (0, 0)),
        ],
        out_specs=pl.BlockSpec((32, RB, CB), lambda i: (i, 0, 0)),
        out_shape=jax.ShapeDtypeStruct((64, RB, CB), jnp.bfloat16),
        cost_estimate=pl.CostEstimate(flops=4 * T * ROWS * 2 * KH, bytes_accessed=10 << 20, transcendentals=0),
        compiler_params=pltpu.CompilerParams(vmem_limit_bytes=48 << 20),
        name="grad",
    )(a, b, ka, kb)


def sum_kernel(in_ref, out_ref):
    total = in_ref[0].astype(jnp.float32)
    for k in range(1, in_ref.shape[0]):
        total += in_ref[k].astype(jnp.float32)
    total = total.astype(jnp.bfloat16)
    for k in range(out_ref.shape[0]):
        out_ref[k] = total


def sum_call(blocks):
    n, tm = blocks.shape[0], 48
    return pl.pallas_call(
        sum_kernel,
        grid=(RB // tm,),
        in_specs=[pl.BlockSpec((n, tm, CB), lambda i: (0, i, 0))],
        out_specs=pl.BlockSpec((32, tm, CB), lambda i: (0, i, 0)),
        out_shape=jax.ShapeDtypeStruct((32, RB, CB), jnp.bfloat16),
        cost_estimate=pl.CostEstimate(flops=n * RB * CB, bytes_accessed=7 << 20, transcendentals=0),
        name="total",
    )(blocks)


def adam_kernel(g_ref, mc_ref, me_ref, vc_ref, ve_ref, step_ref, mr_ref, ms_ref, vr_ref, vs_ref):
    m_unit = jnp.exp2(me_ref[...].astype(jnp.float32)) / 127.0
    v_unit = jnp.exp2(ve_ref[...].astype(jnp.float32)) / 255.0
    for cb in range(4):
        cols = slice(cb * CB, (cb + 1) * CB)
        g = g_ref[cb].astype(jnp.float32)
        m = 0.9 * (mc_ref[:, cols].astype(jnp.float32) * m_unit[:, cb:cb + 1]) + 0.1 * g
        v = 0.999 * (vc_ref[:, cols].astype(jnp.float32) * v_unit[:, cb:cb + 1]) + 0.001 * g * g
        step_ref[:, cols] = m / bias_first / (jnp.sqrt(v / bias_second) + 1e-08)
        ms = jnp.max(jnp.abs(m), axis=1, keepdims=True)
        vs = jnp.max(v, axis=1, keepdims=True)
        ms_ref[:, cb:cb + 1] = ms
        vs_ref[:, cb:cb + 1] = vs
        mr_ref[:, cols] = (m * (1.0 / (ms + 1e-06))).astype(jnp.bfloat16)
        vr_ref[:, cols] = (v * (1.0 / (vs + 1e-06))).astype(jnp.bfloat16)


def adam_call(g, mc, me, vc, ve):
    wide = pl.BlockSpec((RB, KH), lambda i: (i, 0))
    thin = pl.BlockSpec((RB, 4), lambda i: (i, 0))
    return pl.pallas_call(
        adam_kernel,
        grid=(ROWS // RB,),
        in_specs=[pl.BlockSpec((4, RB, CB), lambda i: (i, 0, 0)), wide, thin, wide, thin],
        out_specs=[wide, wide, thin, wide, thin],
        out_shape=[
            jax.ShapeDtypeStruct((ROWS, KH), jnp.float32),
            jax.ShapeDtypeStruct((ROWS, KH), jnp.bfloat16),
            jax.ShapeDtypeStruct((ROWS, 4), jnp.float32),
            jax.ShapeDtypeStruct((ROWS, KH), jnp.bfloat16),
            jax.ShapeDtypeStruct((ROWS, 4), jnp.float32),
        ],
        cost_estimate=pl.CostEstimate(flops=20 * ROWS * KH, bytes_accessed=17 << 20, transcendentals=2 * ROWS * KH),
        name="adam",
    )(g, mc, me, vc, ve)


def device_step(tokens, gain, key_grad, weight, m_code, m_exp, v_code, v_exp):
    zh, c = lax.axis_index("zh"), lax.axis_index("c")
    y, x = lax.axis_index("y"), lax.axis_index("x")
    core = c.astype(jnp.int32).reshape(1)
    gain_row = gain.reshape(1, D)

    mine_q = jnp.where(c == 0, x, y)
    their_q = jnp.where(c == 0, y, x)
    quarter = lax.dynamic_slice(weight, (0, mine_q * CB), (ROWS, CB))
    quarter = send(quarter, across)
    kg_other = send(key_grad, partner)
    w_other = send(weight, partner)

    mine, theirs, inv = norm_call(core, tokens, gain_row)
    received = send(theirs, partner)
    blocks = grad_call(mine, received, key_grad, kg_other)

    ring = [quarter] + [send(quarter, around(k)) for k in (1, 3, 2)]
    ring_other = [send(piece, partner) for piece in ring]
    full = jnp.zeros((D, KH), jnp.bfloat16)
    full = lax.dynamic_update_slice(full, weight, ((2 * zh + c) * ROWS, 0))
    full = lax.dynamic_update_slice(full, w_other, ((2 * zh + 1 - c) * ROWS, 0))
    for k, piece, piece_other in zip((0, 1, 3, 2), ring, ring_other):
        at = lax.rem(mine_q + 4 - k, 4) * CB
        full = lax.dynamic_update_slice(full, piece, ((2 * (1 - zh) + c) * ROWS, at))
        at = lax.rem(their_q + 4 - k, 4) * CB
        full = lax.dynamic_update_slice(full, piece_other, ((2 * (1 - zh) + 1 - c) * ROWS, at))

    blocks = lax.all_to_all(blocks, CHIPS, 0, 0, tiled=True)
    total = sum_call(blocks)
    total = lax.all_to_all(total, REPLICAS, 0, 0, tiled=True)
    step, m_rel, m_scale, v_rel, v_scale = adam_call(total, m_code, m_exp, v_code, v_exp)

    xf = tokens.astype(jnp.float32)
    normed = (xf * inv * gain_row).astype(jnp.bfloat16)
    keys = jnp.dot(normed, full, preferred_element_type=jnp.float32).astype(jnp.bfloat16)
    dnormed = lax.dot_general(key_grad, full, (((1,), (1,)), ((), ())), preferred_element_type=jnp.float32)
    scaled = dnormed * gain_row
    inner = jnp.mean(scaled * xf, axis=1, keepdims=True)
    token_grad = (inv * scaled - xf * (inv * inv * inv * inner)).astype(jnp.bfloat16)
    return keys, token_grad, step, m_rel, m_scale, v_rel, v_scale


def solution(mesh):
    inner = Mesh(mesh.devices.reshape(2, 2, 4, 4, 2), AXES)
    tok = P(AXES, None)
    row = P(("zh", "c"), None)
    return jax.shard_map(
        device_step,
        mesh=inner,
        in_specs=(tok, P(None), tok, row, row, row, row, row),
        out_specs=(tok, tok, row, row, row, row, row),
        check_vma=False,
    )
```

```python
import jax
import jax.numpy as jnp
from jax import lax
from jax.experimental import pallas as pl
from jax.experimental.pallas import tpu as pltpu
from jax.sharding import Mesh, PartitionSpec as P


bias_first = 0.9999734386011124
bias_second = 0.0952078528862904

AXES = ("zh", "c", "y", "x", "zl")

D = 4608
KH = 1024
ROWS = 1152
T = 384
RING = (0, 1, 3, 2)
RB, CB = 144, 256


def index_of(zh, c, y, x, zl):
    return (((zh * 2 + c) * 4 + y) * 4 + x) * 2 + zl


def pairs(move):
    out = []
    for zh in range(2):
        for c in range(2):
            for y in range(4):
                for x in range(4):
                    for zl in range(2):
                        to = move(zh, c, y, x, zl)
                        out.append((index_of(zh, c, y, x, zl), index_of(*to)))
    return out


def partner(zh, c, y, x, zl):
    return zh, 1 - c, y, x, zl


def across(zh, c, y, x, zl):
    return 1 - zh, c, y, x, 1 - zl


def zl_partner(zh, c, y, x, zl):
    return zh, c, y, x, 1 - zl


def opposite(zh, c, y, x, zl):
    return 1 - zh, c, y, x, zl


def around(step, second=False):
    def move(zh, c, y, x, zl):
        if (c == 0) != second:
            return zh, c, y, (x + step) % 4, zl
        return zh, c, (y + step) % 4, x, zl

    return move


def send(value, move):
    return lax.ppermute(value, AXES, pairs(move))


def send_ring(value, second):
    return [send(value, around(k, second)) for k in RING[1:]]


def unpack(where):
    w = where[0]
    return w % 2, (w // 2) % 2, (w // 4) % 4, w // 16


def vmem(n):
    return [pl.BlockSpec(memory_space=pltpu.VMEM)] * n


def norm_kernel(where, x_ref, gain_ref, mine_ref, theirs_ref, inv_ref):
    x = x_ref[...].astype(jnp.float32)
    inv = lax.rsqrt(jnp.mean(x * x, axis=1, keepdims=True) + 1e-06)
    inv_ref[...] = inv
    c = unpack(where)[0]
    for half in range(2):
        for out, which in ((mine_ref, c), (theirs_ref, 1 - c)):
            for part in range(ROWS // 128):
                at = (half * 2 + which) * (ROWS // 128) + part
                cols = pl.ds(pl.multiple_of(at * 128, 128), 128)
                value = x_ref[:, cols].astype(jnp.float32) * inv * gain_ref[pl.ds(at, 1), :]
                out[:, half * ROWS + part * 128:half * ROWS + (part + 1) * 128] = value.astype(jnp.bfloat16)


def norm_call(where, tokens, gain):
    tm = 64
    return pl.pallas_call(
        norm_kernel,
        grid_spec=pltpu.PrefetchScalarGridSpec(
            num_scalar_prefetch=1,
            grid=(T // tm,),
            in_specs=[
                pl.BlockSpec((tm, D), lambda i, where: (i, 0)),
                pl.BlockSpec((D // 128, 128), lambda i, where: (0, 0)),
            ],
            out_specs=[
                pl.BlockSpec((tm, D // 2), lambda i, where: (i, 0)),
                pl.BlockSpec((tm, D // 2), lambda i, where: (i, 0)),
                pl.BlockSpec((tm, 1), lambda i, where: (i, 0)),
            ],
        ),
        out_shape=[
            jax.ShapeDtypeStruct((T, D // 2), jnp.bfloat16),
            jax.ShapeDtypeStruct((T, D // 2), jnp.bfloat16),
            jax.ShapeDtypeStruct((T, 1), jnp.float32),
        ],
        cost_estimate=pl.CostEstimate(flops=6 * T * D, bytes_accessed=4 * T * D, transcendentals=T),
        compiler_params=pltpu.CompilerParams(vmem_limit_bytes=16 << 20),
        name="norm",
    )(where, tokens, gain)


def grad_kernel(where, a_ref, b_ref, ka_ref, kb_ref, *rest):
    outs, hold = rest[:4], rest[4]
    dims = (((0,), (0,)), ((), ()))
    acc = lax.dot_general(a_ref[...], ka_ref[...], dims, preferred_element_type=jnp.float32)
    acc += lax.dot_general(b_ref[...], kb_ref[...], dims, preferred_element_type=jnp.float32)
    hold[...] = acc.astype(jnp.bfloat16)
    _, _, pos, other = unpack(where)
    for k in range(4):
        first = lax.rem(pos + k, 4) * (2 * RB)
        for j in range(4):
            o = lax.rem(other + j, 4)
            rows = pl.ds(pl.multiple_of(first + (o // 2) * RB, 16), RB)
            for zl in range(2):
                cols = pl.ds(pl.multiple_of((o % 2) * (2 * CB) + zl * CB, 128), CB)
                outs[k][j, 0, zl] = hold[rows, cols]


def grad_call(where, a, b, ka, kb):
    return pl.pallas_call(
        grad_kernel,
        grid_spec=pltpu.PrefetchScalarGridSpec(
            num_scalar_prefetch=1,
            grid=(2,),
            in_specs=[
                pl.BlockSpec((T, ROWS), lambda i, where: (0, i)),
                pl.BlockSpec((T, ROWS), lambda i, where: (0, i)),
                pl.BlockSpec((T, KH), lambda i, where: (0, 0)),
                pl.BlockSpec((T, KH), lambda i, where: (0, 0)),
            ],
            out_specs=[pl.BlockSpec((4, 1, 2, RB, CB), lambda i, where: (0, i, 0, 0, 0))] * 4,
            scratch_shapes=[pltpu.VMEM((ROWS, KH), jnp.bfloat16)],
        ),
        out_shape=[jax.ShapeDtypeStruct((4, 2, 2, RB, CB), jnp.bfloat16)] * 4,
        cost_estimate=pl.CostEstimate(flops=4 * T * ROWS * 2 * KH, bytes_accessed=10 << 20, transcendentals=0),
        compiler_params=pltpu.CompilerParams(vmem_limit_bytes=26 << 20),
        name="grad",
    )(where, a, b, ka, kb)


def add_up(refs):
    total = refs[0][...].astype(jnp.float32)
    for ref in refs[1:]:
        total += ref[...].astype(jnp.float32)
    return total.astype(jnp.bfloat16)


def first_sum_kernel(*refs):
    for j in range(4):
        refs[4 + j][...] = add_up([ref.at[j] for ref in refs[:4]])


def first_sum(parts):
    return pl.pallas_call(
        first_sum_kernel,
        in_specs=vmem(4),
        out_specs=vmem(4),
        out_shape=[jax.ShapeDtypeStruct((2, 2, RB, CB), jnp.bfloat16)] * 4,
        cost_estimate=pl.CostEstimate(flops=64 * RB * CB, bytes_accessed=6 << 20, transcendentals=0),
        compiler_params=pltpu.CompilerParams(vmem_limit_bytes=16 << 20),
        name="first_sum",
    )(*parts)


def second_sum_kernel(where, *refs):
    zh = unpack(where)[1]
    for out, h in ((refs[4], zh), (refs[5], 1 - zh)):
        out[...] = add_up([ref.at[h] for ref in refs[:4]])


def second_sum(where, parts):
    return pl.pallas_call(
        second_sum_kernel,
        in_specs=[pl.BlockSpec(memory_space=pltpu.SMEM)] + vmem(4),
        out_specs=vmem(2),
        out_shape=[jax.ShapeDtypeStruct((2, RB, CB), jnp.bfloat16)] * 2,
        cost_estimate=pl.CostEstimate(flops=16 * RB * CB, bytes_accessed=2 << 20, transcendentals=0),
        compiler_params=pltpu.CompilerParams(vmem_limit_bytes=8 << 20),
        name="second_sum",
    )(where, *parts)


def total_kernel(own, near, across_z, far, out):
    near_sum = own[...].astype(jnp.float32) + near[...].astype(jnp.float32)
    far_sum = across_z[...].astype(jnp.float32) + far[...].astype(jnp.float32)
    out[...] = (near_sum + far_sum).astype(jnp.bfloat16)


def total_call(*parts):
    return pl.pallas_call(
        total_kernel,
        in_specs=vmem(4),
        out_specs=vmem(1)[0],
        out_shape=jax.ShapeDtypeStruct((2, RB, CB), jnp.bfloat16),
        cost_estimate=pl.CostEstimate(flops=8 * RB * CB, bytes_accessed=1 << 20, transcendentals=0),
        compiler_params=pltpu.CompilerParams(vmem_limit_bytes=8 << 20),
        name="total",
    )(*parts)


def join_kernel(*refs):
    for k, ref in zip(RING, refs[:4]):
        refs[4][k] = ref[...]


def join_call(parts):
    return pl.pallas_call(
        join_kernel,
        in_specs=vmem(4),
        out_specs=vmem(1)[0],
        out_shape=jax.ShapeDtypeStruct((4, 2, RB, CB), jnp.bfloat16),
        cost_estimate=pl.CostEstimate(flops=0, bytes_accessed=1 << 20, transcendentals=0),
        compiler_params=pltpu.CompilerParams(vmem_limit_bytes=8 << 20),
        name="join",
    )(*parts)


def adam_rows(other, rb, read, mc_ref, vc_ref, unit_ref, step_ref, mr_ref, vr_ref, keep_scale):
    for cb in range(4):
        cols = slice(cb * CB, (cb + 1) * CB)
        back = lax.rem(other + 4 - (rb * 2 + cb // 2), 4)
        g = read(back, cb % 2).astype(jnp.float32)
        m = mc_ref[:, cols].astype(jnp.float32) * unit_ref[:, cb:cb + 1] + 0.1 * g
        v = vc_ref[:, cols].astype(jnp.float32) * unit_ref[:, 4 + cb:5 + cb] + 0.001 * g * g
        w = v * (bias_first * bias_first / bias_second)
        step_ref[:, cols] = m / (w * lax.rsqrt(w) + 1e-08 * bias_first)
        ms = jnp.max(jnp.abs(m), axis=1, keepdims=True)
        vs = jnp.max(v, axis=1, keepdims=True)
        keep_scale(cb, ms, vs)
        mr_ref[:, cols] = (m * (1.0 / (ms + 1e-06))).astype(jnp.bfloat16)
        vr_ref[:, cols] = (v * (1.0 / (vs + 1e-06))).astype(jnp.bfloat16)


def units_kernel(me_ref, ve_ref, out_ref, hold):
    hold[...] = jnp.zeros_like(hold)
    for part in range(ROWS // 128):
        rows = slice(part * 128, (part + 1) * 128)
        hold[0:4, :] = jnp.exp2(me_ref[:, rows].astype(jnp.float32)) * (0.9 / 127.0)
        hold[4:8, :] = jnp.exp2(ve_ref[:, rows].astype(jnp.float32)) * (0.999 / 255.0)
        out_ref[rows, :] = hold[...].T


def units_call(m_exp, v_exp):
    return pl.pallas_call(
        units_kernel,
        in_specs=vmem(2),
        out_specs=vmem(1)[0],
        out_shape=jax.ShapeDtypeStruct((ROWS, 128), jnp.float32),
        scratch_shapes=[pltpu.VMEM((128, 128), jnp.float32)],
        cost_estimate=pl.CostEstimate(flops=ROWS * 128, bytes_accessed=1 << 20, transcendentals=8 * ROWS),
        compiler_params=pltpu.CompilerParams(vmem_limit_bytes=4 << 20),
        name="units",
    )(m_exp.T, v_exp.T)


def adam_own_kernel(where, g_ref, mc_ref, vc_ref, unit_ref, step_ref, mr_ref, vr_ref, scale_ref):
    def keep_scale(cb, ms, vs):
        scale_ref[:, cb:cb + 1] = ms
        scale_ref[:, 4 + cb:5 + cb] = vs

    adam_rows(
        unpack(where)[3], pl.program_id(0), lambda back, zl: g_ref[back, zl],
        mc_ref, vc_ref, unit_ref, step_ref, mr_ref, vr_ref, keep_scale,
    )


WIDE = [
    jax.ShapeDtypeStruct((ROWS, KH), jnp.float32),
    jax.ShapeDtypeStruct((ROWS, KH), jnp.bfloat16),
    jax.ShapeDtypeStruct((ROWS, KH), jnp.bfloat16),
]


def adam_own(where, g, mc, vc, units):
    def at(i, where):
        return (where[0] // 4) % 4 * 2 + i, 0

    wide, thin = pl.BlockSpec((RB, KH), at), pl.BlockSpec((RB, 128), at)
    return pl.pallas_call(
        adam_own_kernel,
        grid_spec=pltpu.PrefetchScalarGridSpec(
            num_scalar_prefetch=1,
            grid=(2,),
            in_specs=[pl.BlockSpec((4, 2, RB, CB), lambda i, where: (0, 0, 0, 0)), wide, wide, thin],
            out_specs=[wide, wide, wide, pl.BlockSpec((RB, 128), lambda i, where: (i, 0))],
        ),
        out_shape=WIDE + [jax.ShapeDtypeStruct((2 * RB, 128), jnp.float32)],
        cost_estimate=pl.CostEstimate(flops=5 * ROWS * KH, bytes_accessed=4 << 20, transcendentals=ROWS * KH // 2),
        compiler_params=pltpu.CompilerParams(vmem_limit_bytes=16 << 20),
        name="adam_own",
    )(where, g, mc, vc, units)


def place_of(i, pos):
    k = jnp.where(i < 2, 1, jnp.where(i < 4, 3, 2))
    return lax.rem(pos + 4 - k, 4)


def adam_rest_kernel(where, g1, g3, g2, mc_ref, vc_ref, unit_ref, s0, *rest):
    step_ref, mr_ref, vr_ref, ms_ref, vs_ref, scales = rest[3:]
    _, _, pos, other = unpack(where)
    i = pl.program_id(0)
    rb = lax.rem(i, 2)
    rows = pl.ds(pl.multiple_of(place_of(i, pos) * (2 * RB) + rb * RB, 8), RB)

    @pl.when(i == 0)
    def _():
        scales[pl.ds(pl.multiple_of(pos * (2 * RB), 8), 2 * RB), :] = s0[...]

    def keep_scale(cb, ms, vs):
        scales[rows, cb:cb + 1] = ms
        scales[rows, 4 + cb:5 + cb] = vs

    def read(back, zl):
        return jnp.where(i < 2, g1[back, zl], jnp.where(i < 4, g3[back, zl], g2[back, zl]))

    adam_rows(other, rb, read, mc_ref, vc_ref, unit_ref, step_ref, mr_ref, vr_ref, keep_scale)

    @pl.when(i == 5)
    def _():
        for part in range(ROWS // 128):
            cols = slice(part * 128, (part + 1) * 128)
            turned = scales[cols, :].T
            ms_ref[:, cols] = turned[0:4, :]
            vs_ref[:, cols] = turned[4:8, :]


def adam_rest(where, g, mc, vc, units, s0, done):
    def at(i, where):
        return place_of(i, (where[0] // 4) % 4) * 2 + lax.rem(i, 2), 0

    wide, thin = pl.BlockSpec((RB, KH), at), pl.BlockSpec((RB, 128), at)
    flat = pl.BlockSpec((4, ROWS), lambda i, where: (0, 0))
    whole = pl.BlockSpec((4, 2, RB, CB), lambda i, where: (0, 0, 0, 0))
    return pl.pallas_call(
        adam_rest_kernel,
        grid_spec=pltpu.PrefetchScalarGridSpec(
            num_scalar_prefetch=1,
            grid=(6,),
            in_specs=[whole] * 3 + [wide, wide, thin, pl.BlockSpec((2 * RB, 128), lambda i, where: (0, 0))]
            + [pl.BlockSpec(memory_space=pl.ANY)] * 3,
            out_specs=[wide, wide, wide, flat, flat],
            scratch_shapes=[pltpu.VMEM((ROWS, 128), jnp.float32)],
        ),
        out_shape=WIDE + [jax.ShapeDtypeStruct((4, ROWS), jnp.float32)] * 2,
        input_output_aliases={8: 0, 9: 1, 10: 2},
        cost_estimate=pl.CostEstimate(flops=15 * ROWS * KH, bytes_accessed=12 << 20, transcendentals=2 * ROWS * KH),
        compiler_params=pltpu.CompilerParams(vmem_limit_bytes=24 << 20),
        name="adam_rest",
    )(where, *g, mc, vc, units, s0, *done)


def dot(a, b):
    return jnp.dot(a, b, preferred_element_type=jnp.float32)


def dot_t(a, b):
    return lax.dot_general(a, b, (((1,), (1,)), ((), ())), preferred_element_type=jnp.float32)


def shard_cols(shard):
    return pl.ds(pl.multiple_of(shard * ROWS, 128), ROWS)


def scale_by_gain(value, gain, shard):
    parts = []
    for part in range(ROWS // 128):
        row = gain[pl.ds(shard * (ROWS // 128) + part, 1), :]
        parts.append(value[:, part * 128:(part + 1) * 128] * row)
    return jnp.concatenate(parts, axis=1)


def half(zh, c, mine, theirs, x, kg, gain, weights, scaled):
    total = dot(mine[:, shard_cols(zh)], weights[0][...]) + dot(theirs[:, shard_cols(zh)], weights[1][...])
    inner = jnp.zeros((T, 1), jnp.float32)
    for k, shard in enumerate((2 * zh + c, 2 * zh + 1 - c)):
        value = scale_by_gain(dot_t(kg[...], weights[k][...]), gain, shard)
        scaled[:, k * ROWS:(k + 1) * ROWS] = value
        inner += jnp.sum(value * x[:, shard_cols(shard)].astype(jnp.float32), axis=1, keepdims=True)
    return total, inner


def near_kernel(where, mine, theirs, x, kg, gain, own, other, keys, inner, scaled):
    c, zh, _, _ = unpack(where)
    keys[...], inner[...] = half(zh, c, mine, theirs, x, kg, gain, (own, other), scaled)


def near_call(where, mine, theirs, tokens, key_grad, gain, own, other):
    return pl.pallas_call(
        near_kernel,
        in_specs=[pl.BlockSpec(memory_space=pltpu.SMEM)] + vmem(7),
        out_specs=vmem(3),
        out_shape=[
            jax.ShapeDtypeStruct((T, KH), jnp.float32),
            jax.ShapeDtypeStruct((T, 1), jnp.float32),
            jax.ShapeDtypeStruct((T, D // 2), jnp.float32),
        ],
        cost_estimate=pl.CostEstimate(flops=2 * T * D * KH, bytes_accessed=18 << 20, transcendentals=0),
        compiler_params=pltpu.CompilerParams(vmem_limit_bytes=30 << 20),
        name="near",
    )(where, mine, theirs, tokens, key_grad, gain, own, other)


def keys_kernel(where, mine, theirs, near, far, far_other, out):
    there = shard_cols(1 - unpack(where)[1])
    total = near[...] + dot(mine[:, there], far[...]) + dot(theirs[:, there], far_other[...])
    out[...] = total.astype(jnp.bfloat16)


def keys_call(where, mine, theirs, near, far, far_other):
    return pl.pallas_call(
        keys_kernel,
        in_specs=[pl.BlockSpec(memory_space=pltpu.SMEM)] + vmem(5),
        out_specs=vmem(1)[0],
        out_shape=jax.ShapeDtypeStruct((T, KH), jnp.bfloat16),
        cost_estimate=pl.CostEstimate(flops=T * D * KH, bytes_accessed=10 << 20, transcendentals=0),
        compiler_params=pltpu.CompilerParams(vmem_limit_bytes=20 << 20),
        name="keys",
    )(where, mine, theirs, near, far, far_other)


def back_kernel(where, x, kg, inv_ref, gain, inner_ref, scaled, far, far_other, out, hold):
    c, zh, _, _ = unpack(where)
    inner = inner_ref[...]
    shards = (2 * (1 - zh) + c, 2 * (1 - zh) + 1 - c)
    for k, (shard, weight) in enumerate(zip(shards, (far, far_other))):
        value = scale_by_gain(dot_t(kg[...], weight[...]), gain, shard)
        hold[:, k * ROWS:(k + 1) * ROWS] = value
        inner += jnp.sum(value * x[:, shard_cols(shard)].astype(jnp.float32), axis=1, keepdims=True)
    inv = inv_ref[...]
    pull = inv * inv * inv * (inner * (1.0 / D))
    for source, shards in ((scaled, (2 * zh + c, 2 * zh + 1 - c)), (hold, shards)):
        for k, shard in enumerate(shards):
            xf = x[:, shard_cols(shard)].astype(jnp.float32)
            value = inv * source[:, k * ROWS:(k + 1) * ROWS] - xf * pull
            out[:, shard_cols(shard)] = value.astype(jnp.bfloat16)


def back_call(where, tokens, key_grad, inv, gain, inner, scaled, far, far_other):
    return pl.pallas_call(
        back_kernel,
        in_specs=[pl.BlockSpec(memory_space=pltpu.SMEM)] + vmem(8),
        out_specs=vmem(1)[0],
        out_shape=jax.ShapeDtypeStruct((T, D), jnp.bfloat16),
        scratch_shapes=[pltpu.VMEM((T, D // 2), jnp.float32)],
        cost_estimate=pl.CostEstimate(flops=T * D * KH, bytes_accessed=16 << 20, transcendentals=0),
        compiler_params=pltpu.CompilerParams(vmem_limit_bytes=32 << 20),
        name="back",
    )(where, tokens, key_grad, inv, gain, inner, scaled, far, far_other)


def device_step(tokens, gain, key_grad, weight, m_code, m_exp, v_code, v_exp):
    zh, c = lax.axis_index("zh"), lax.axis_index("c")
    y, x = lax.axis_index("y"), lax.axis_index("x")
    pos = jnp.where(c == 0, x, y)
    pos_other = jnp.where(c == 0, y, x)
    where = (c + 2 * zh + 4 * pos + 16 * pos_other).astype(jnp.int32).reshape(1)

    gain = gain.reshape(D // 128, 128)

    far = send(weight, across)
    kg_other = send(key_grad, partner)
    w_other = send(weight, partner)

    mine, theirs, inv = norm_call(where, tokens, gain)
    received = send(theirs, partner)
    parts = grad_call(where, mine, received, key_grad, kg_other)
    parts = [parts[0]] + [send(parts[k], around(k)) for k in RING[1:]]
    near_keys, inner, scaled = near_call(where, mine, theirs, tokens, key_grad, gain, weight, w_other)
    units = units_call(m_exp, v_exp)
    parts = list(first_sum(parts))
    far_other = send(far, partner)
    parts = [parts[0]] + [send(parts[k], around(k, True)) for k in RING[1:]]
    keys = keys_call(where, mine, theirs, near_keys, far, far_other)
    keep, give = second_sum(where, parts)
    near = send(keep, zl_partner)
    across_z = send(give, across)
    opposite_z = send(give, opposite)
    total = total_call(keep, near, across_z, opposite_z)

    total = join_call([total] + send_ring(total, True))
    got = send_ring(total, False)
    *done, scales = adam_own(where, total, m_code, v_code, units)
    token_grad = back_call(where, tokens, key_grad, inv, gain, inner, scaled, far, far_other)
    outs = adam_rest(where, got, m_code, v_code, units, scales, done)
    step, m_rel, v_rel, m_scale, v_scale = outs
    return keys, token_grad, step, m_rel, m_scale.T, v_rel, v_scale.T


def solution(mesh):
    inner = Mesh(mesh.devices.reshape(2, 2, 4, 4, 2), AXES)
    tok = P(AXES, None)
    row = P(("zh", "c"), None)

    return jax.shard_map(
        device_step,
        mesh=inner,
        in_specs=(tok, P(None), tok, row, row, row, row, row),
        out_specs=(tok, tok, row, row, row, row, row),
        check_vma=False,
    )
```

```python
import functools

import jax
import jax.numpy as jnp
from jax import lax
from jax.experimental import pallas as pl
from jax.experimental.pallas import tpu as pltpu
from jax.sharding import Mesh, PartitionSpec as P


bias_first = 0.9999734386011124
bias_second = 0.0952078528862904

AXES = ("zh", "c", "y", "x", "zl")

D = 4608
KH = 1024
ROWS = 1152
T = 384
RING = (0, 1, 3, 2)
RB, CB = 144, 256


def index_of(zh, c, y, x, zl):
    return (((zh * 2 + c) * 4 + y) * 4 + x) * 2 + zl


def pairs(move):
    out = []
    for zh in range(2):
        for c in range(2):
            for y in range(4):
                for x in range(4):
                    for zl in range(2):
                        to = move(zh, c, y, x, zl)
                        out.append((index_of(zh, c, y, x, zl), index_of(*to)))
    return out


def partner(zh, c, y, x, zl):
    return zh, 1 - c, y, x, zl


def across(zh, c, y, x, zl):
    return 1 - zh, c, y, x, 1 - zl


def zl_partner(zh, c, y, x, zl):
    return zh, c, y, x, 1 - zl


def opposite(zh, c, y, x, zl):
    return 1 - zh, c, y, x, zl


def around(step, second=False):
    def move(zh, c, y, x, zl):
        if (c == 0) != second:
            return zh, c, y, (x + step) % 4, zl
        return zh, c, (y + step) % 4, x, zl

    return move


def send(value, move):
    return lax.ppermute(value, AXES, pairs(move))


def send_ring(value, second):
    return [send(value, around(k, second)) for k in RING[1:]]


def unpack(where):
    w = where[0]
    return w % 2, (w // 2) % 2, (w // 4) % 4, w // 16


def vmem(n):
    return [pl.BlockSpec(memory_space=pltpu.VMEM)] * n


STEP = 64


def norm_columns(x, inv, gain, core, rows, out):
    for half in range(2):
        for part in range(ROWS // 128):
            at = (half * 2 + core) * (ROWS // 128) + part
            cols = pl.ds(pl.multiple_of(at * 128, 128), 128)
            value = x[rows, cols].astype(jnp.float32) * inv[rows, :] * gain[pl.ds(at, 1), :]
            out[rows, half * ROWS + part * 128:half * ROWS + (part + 1) * 128] = value.astype(jnp.bfloat16)


def norm_kernel(where, x_hbm, gain_hbm, theirs, inv, x, gain, sems):
    rows = [slice(k * STEP, (k + 1) * STEP) for k in range(T // STEP)]
    copies = [pltpu.make_async_copy(x_hbm.at[r], x.at[r], sems.at[k]) for k, r in enumerate(rows)]
    gain_copy = pltpu.make_async_copy(gain_hbm, gain, sems.at[len(rows)])
    gain_copy.start()
    for copy in copies:
        copy.start()
    gain_copy.wait()
    c = unpack(where)[0]
    for copy, r in zip(copies, rows):
        copy.wait()
        xf = x[r, :].astype(jnp.float32)
        inv[r, :] = lax.rsqrt(jnp.mean(xf * xf, axis=1, keepdims=True) + 1e-06)
        norm_columns(x, inv, gain, 1 - c, r, theirs)


def norm_call(where, tokens, gain):
    return pl.pallas_call(
        norm_kernel,
        in_specs=[pl.BlockSpec(memory_space=pltpu.SMEM)] + [pl.BlockSpec(memory_space=pl.ANY)] * 2,
        out_specs=vmem(4),
        out_shape=[
            jax.ShapeDtypeStruct((T, D // 2), jnp.bfloat16),
            jax.ShapeDtypeStruct((T, 1), jnp.float32),
            jax.ShapeDtypeStruct((T, D), jnp.bfloat16),
            jax.ShapeDtypeStruct((D // 128, 128), jnp.float32),
        ],
        scratch_shapes=[pltpu.SemaphoreType.DMA((T // STEP + 1,))],
        cost_estimate=pl.CostEstimate(flops=4 * T * D, bytes_accessed=4 * T * D, transcendentals=T),
        compiler_params=pltpu.CompilerParams(vmem_limit_bytes=47 << 20),
        name="norm",
    )(where, tokens, gain)


def flip(in_ref, out_ref):
    for part in range(D // 2 // 128):
        cols = slice(part * 128, (part + 1) * 128)
        out_ref[cols, :] = in_ref[:, cols].T


def mine_kernel(where, x, inv, gain, mine, mine_t):
    for k in range(T // STEP):
        norm_columns(x, inv, gain, unpack(where)[0], slice(k * STEP, (k + 1) * STEP), mine)
    flip(mine, mine_t)


def mine_call(where, tokens, inv, gain):
    return pl.pallas_call(
        mine_kernel,
        in_specs=[pl.BlockSpec(memory_space=pltpu.SMEM)] + vmem(3),
        out_specs=vmem(2),
        out_shape=[
            jax.ShapeDtypeStruct((T, D // 2), jnp.bfloat16),
            jax.ShapeDtypeStruct((D // 2, T), jnp.bfloat16),
        ],
        cost_estimate=pl.CostEstimate(flops=2 * T * D, bytes_accessed=3 * T * D, transcendentals=0),
        compiler_params=pltpu.CompilerParams(vmem_limit_bytes=6 << 20),
        name="mine",
    )(where, tokens, inv, gain)


def grad_columns(where, a_ref, b_ref, ka_ref, kb_ref, k, out):
    _, _, pos, other = unpack(where)
    cols = pl.ds(pl.multiple_of(lax.rem(pos + k, 4) * CB, 128), CB)
    for zh in range(2):
        rows = slice(zh * ROWS, (zh + 1) * ROWS)
        acc = dot(a_ref[rows, :], ka_ref[:, cols]) + dot(b_ref[rows, :], kb_ref[:, cols])
        for o in range(4):
            for zl in range(2):
                at = (o * 2 + zl) * RB
                out[lax.rem(o + 4 - other, 4), zh, zl] = acc[at:at + RB, :].astype(out.dtype)


def first_grad_kernel(where, a_ref, b_in, ka_ref, kb_ref, b_ref, out):
    flip(b_in, b_ref)
    grad_columns(where, a_ref, b_ref, ka_ref, kb_ref, 2, out)


def grad_kernel(ks, where, *refs):
    for k, out in zip(ks, refs[4:]):
        grad_columns(where, *refs[:4], k, out)


def grad_call(ks, where, a, b, ka, kb, dtype=jnp.bfloat16, first=False):
    out = [jax.ShapeDtypeStruct((4, 2, 2, RB, CB), dtype)] * len(ks)
    return pl.pallas_call(
        first_grad_kernel if first else functools.partial(grad_kernel, ks),
        in_specs=[pl.BlockSpec(memory_space=pltpu.SMEM)] + vmem(4),
        out_specs=vmem(len(ks) + first),
        out_shape=[jax.ShapeDtypeStruct((D // 2, T), jnp.bfloat16)] * first + out,
        cost_estimate=pl.CostEstimate(flops=T * D * KH // 2 * len(ks), bytes_accessed=6 << 20, transcendentals=0),
        compiler_params=pltpu.CompilerParams(vmem_limit_bytes=8 << 20),
        name="grad",
    )(where, a, b, ka, kb)


def add_up(refs):
    total = refs[0][...].astype(jnp.float32)
    for ref in refs[1:]:
        total += ref[...].astype(jnp.float32)
    return total


def first_sum_kernel(*refs):
    for j in range(4):
        refs[4 + j][...] = add_up([ref.at[j] for ref in refs[:4]]).astype(refs[4 + j].dtype)


def first_sum(parts):
    return pl.pallas_call(
        first_sum_kernel,
        in_specs=vmem(4),
        out_specs=vmem(4),
        out_shape=[jax.ShapeDtypeStruct((2, 2, RB, CB), kind) for kind in (jnp.float32,) + (jnp.bfloat16,) * 3],
        cost_estimate=pl.CostEstimate(flops=64 * RB * CB, bytes_accessed=6 << 20, transcendentals=0),
        compiler_params=pltpu.CompilerParams(vmem_limit_bytes=8 << 20),
        name="first_sum",
    )(*parts)


def second_sum_kernel(where, *refs):
    zh = unpack(where)[1]
    for out, h in ((refs[4], zh), (refs[5], 1 - zh)):
        out[...] = add_up([ref.at[h] for ref in refs[:4]]).astype(jnp.bfloat16)


def second_sum(where, parts):
    return pl.pallas_call(
        second_sum_kernel,
        in_specs=[pl.BlockSpec(memory_space=pltpu.SMEM)] + vmem(4),
        out_specs=vmem(2),
        out_shape=[jax.ShapeDtypeStruct((2, RB, CB), jnp.bfloat16)] * 2,
        cost_estimate=pl.CostEstimate(flops=16 * RB * CB, bytes_accessed=2 << 20, transcendentals=0),
        compiler_params=pltpu.CompilerParams(vmem_limit_bytes=4 << 20),
        name="second_sum",
    )(where, *parts)


def total_kernel(own, near, across_z, far, out):
    near_sum = own[...].astype(jnp.float32) + near[...].astype(jnp.float32)
    far_sum = across_z[...].astype(jnp.float32) + far[...].astype(jnp.float32)
    out[...] = (near_sum + far_sum).astype(jnp.bfloat16)


def total_call(*parts):
    return pl.pallas_call(
        total_kernel,
        in_specs=vmem(4),
        out_specs=vmem(1)[0],
        out_shape=jax.ShapeDtypeStruct((2, RB, CB), jnp.bfloat16),
        cost_estimate=pl.CostEstimate(flops=8 * RB * CB, bytes_accessed=1 << 20, transcendentals=0),
        compiler_params=pltpu.CompilerParams(vmem_limit_bytes=4 << 20),
        name="total",
    )(*parts)


def join_kernel(*refs):
    for k, ref in zip(RING, refs[:4]):
        refs[4][k] = ref[...]


def join_call(parts):
    return pl.pallas_call(
        join_kernel,
        in_specs=vmem(4),
        out_specs=vmem(1)[0],
        out_shape=jax.ShapeDtypeStruct((4, 2, RB, CB), jnp.bfloat16),
        cost_estimate=pl.CostEstimate(flops=0, bytes_accessed=1 << 20, transcendentals=0),
        compiler_params=pltpu.CompilerParams(vmem_limit_bytes=4 << 20),
        name="join",
    )(*parts)


SCALE = bias_first * bias_first / bias_second


def old_kernel(me_ref, ve_ref, mc_ref, vc_ref, m_ref, w_ref, hold):
    hold[...] = jnp.zeros_like(hold)
    for part in range(ROWS // 128):
        rows = slice(part * 128, (part + 1) * 128)
        hold[0:4, :] = jnp.exp2(me_ref[:, rows].astype(jnp.float32)) * (0.9 / 127.0)
        hold[4:8, :] = jnp.exp2(ve_ref[:, rows].astype(jnp.float32)) * (0.999 * SCALE / 255.0)
        unit = hold[...].T
        for cb in range(4):
            cols = slice(cb * CB, (cb + 1) * CB)
            m_ref[rows, cols] = mc_ref[rows, cols].astype(jnp.float32) * unit[:, cb:cb + 1]
            w_ref[rows, cols] = vc_ref[rows, cols].astype(jnp.float32) * unit[:, 4 + cb:5 + cb]


def old_call(m_exp, v_exp, m_code, v_code):
    return pl.pallas_call(
        old_kernel,
        in_specs=vmem(4),
        out_specs=vmem(2),
        out_shape=[jax.ShapeDtypeStruct((ROWS, KH), jnp.float32)] * 2,
        scratch_shapes=[pltpu.VMEM((128, 128), jnp.float32)],
        cost_estimate=pl.CostEstimate(flops=4 * ROWS * KH, bytes_accessed=14 << 20, transcendentals=8 * ROWS),
        compiler_params=pltpu.CompilerParams(vmem_limit_bytes=12 << 20),
        name="old",
    )(m_exp.T, v_exp.T, m_code, v_code)


def adam_rows(other, half, read, m_old, w_old, step_ref, mr_ref, vr_ref, keep_scale):
    lane = lax.broadcasted_iota(jnp.int32, (RB, 128), 1)
    for b in range(4):
        rows = slice(b * RB, (b + 1) * RB)
        back = lax.rem(other + 8 - (2 * half + b // 2), 4)
        g = read(back, b % 2).astype(jnp.float32)
        m = m_old[rows, :] + 0.1 * g
        w = w_old[rows, :] + (0.001 * SCALE) * (g * g)
        step_ref[rows, :] = m / (w * lax.rsqrt(w) + 1e-08 * bias_first)
        ms = jnp.max(jnp.abs(m), axis=1, keepdims=True)
        vs = jnp.max(w, axis=1, keepdims=True) * (1.0 / SCALE)
        keep_scale(b, lane, ms, vs)
        mr_ref[rows, :] = (m * (1.0 / (ms + 1e-06))).astype(jnp.bfloat16)
        vr_ref[rows, :] = (w * ((1.0 / SCALE) / (vs + 1e-06))).astype(jnp.bfloat16)


def adam_own_kernel(where, g_ref, m_old, w_old, step_ref, mr_ref, vr_ref, scale_ref):
    _, _, p, other = unpack(where)

    def keep_scale(b, lane, ms, vs):
        scale_ref[b * RB:(b + 1) * RB, :] = jnp.where(lane == p, ms, jnp.where(lane == 4 + p, vs, 0.0))

    adam_rows(
        other, pl.program_id(0), lambda back, zl: g_ref[back, zl],
        m_old, w_old, step_ref, mr_ref, vr_ref, keep_scale,
    )


WIDE = [
    jax.ShapeDtypeStruct((ROWS, KH), jnp.float32),
    jax.ShapeDtypeStruct((ROWS, KH), jnp.bfloat16),
    jax.ShapeDtypeStruct((ROWS, KH), jnp.bfloat16),
]


def adam_own(where, g, old):
    wide = pl.BlockSpec((4 * RB, CB), lambda i, where: (i, (where[0] // 4) % 4))
    thin = pl.BlockSpec((4 * RB, 128), lambda i, where: (i, 0))
    return pl.pallas_call(
        adam_own_kernel,
        grid_spec=pltpu.PrefetchScalarGridSpec(
            num_scalar_prefetch=1,
            grid=(2,),
            in_specs=[pl.BlockSpec((4, 2, RB, CB), lambda i, where: (0, 0, 0, 0)), wide, wide],
            out_specs=[wide, wide, wide, thin],
        ),
        out_shape=WIDE + [jax.ShapeDtypeStruct((ROWS, 128), jnp.float32)],
        cost_estimate=pl.CostEstimate(flops=5 * ROWS * KH, bytes_accessed=4 << 20, transcendentals=ROWS * KH // 2),
        compiler_params=pltpu.CompilerParams(vmem_limit_bytes=10 << 20),
        name="adam_own",
    )(where, g, *old)


def place_of(ks, i, pos):
    k = ks[0]
    for n in range(1, len(ks)):
        k = jnp.where(i < 2 * n, k, ks[n])
    return lax.rem(pos + 4 - k, 4)


def adam_more_kernel(ks, last, where, *refs):
    n = len(ks)
    gs, (m_old, w_old, s0) = refs[:n], refs[n:n + 3]
    step_ref, mr_ref, vr_ref = refs[n + 6:n + 9]
    scales = refs[-1]
    _, _, pos, other = unpack(where)
    i = pl.program_id(0)
    p, half = place_of(ks, i, pos), lax.rem(i, 2)

    @pl.when(i == 0)
    def _():
        scales[...] = s0[...]

    def keep_scale(b, lane, ms, vs):
        rows = pl.ds(pl.multiple_of(half * (4 * RB) + b * RB, 8), RB)
        scales[rows, :] = jnp.where(lane == p, ms, jnp.where(lane == 4 + p, vs, scales[rows, :]))

    def read(back, zl):
        g = gs[0][back, zl]
        for k in range(1, n):
            g = jnp.where(i < 2 * k, g, gs[k][back, zl])
        return g

    adam_rows(other, half, read, m_old, w_old, step_ref, mr_ref, vr_ref, keep_scale)

    if last:
        @pl.when(i == 2 * n - 1)
        def _():
            for part in range(ROWS // 128):
                cols = slice(part * 128, (part + 1) * 128)
                turned = scales[cols, :].T
                refs[n + 9][:, cols] = turned[0:4, :]
                refs[n + 10][:, cols] = turned[4:8, :]


def adam_more(ks, last, where, g, old, s0, done):
    n = len(ks)
    wide = pl.BlockSpec((4 * RB, CB), lambda i, where: (lax.rem(i, 2), place_of(ks, i, (where[0] // 4) % 4)))
    flat = pl.BlockSpec((4, ROWS), lambda i, where: (0, 0))
    tall = pl.BlockSpec((ROWS, 128), lambda i, where: (0, 0))
    whole = pl.BlockSpec((4, 2, RB, CB), lambda i, where: (0, 0, 0, 0))
    scale_shapes = [jax.ShapeDtypeStruct((4, ROWS), jnp.float32)] * 2 if last else [jax.ShapeDtypeStruct((ROWS, 128), jnp.float32)]
    return pl.pallas_call(
        functools.partial(adam_more_kernel, ks, last),
        grid_spec=pltpu.PrefetchScalarGridSpec(
            num_scalar_prefetch=1,
            grid=(2 * n,),
            in_specs=[whole] * n + [wide, wide, tall] + [pl.BlockSpec(memory_space=pl.ANY)] * 3,
            out_specs=[wide, wide, wide] + ([flat, flat] if last else [tall]),
            scratch_shapes=[pltpu.VMEM((ROWS, 128), jnp.float32)] * last,
        ),
        out_shape=WIDE + scale_shapes,
        input_output_aliases={n + 4: 0, n + 5: 1, n + 6: 2},
        cost_estimate=pl.CostEstimate(flops=5 * n * ROWS * KH, bytes_accessed=n * (4 << 20), transcendentals=n * ROWS * KH // 2),
        compiler_params=pltpu.CompilerParams(vmem_limit_bytes=12 << 20),
        name="adam_more",
    )(where, *g, *old, s0, *done)


def dot(a, b):
    return jnp.dot(a, b, preferred_element_type=jnp.float32)


def dot_t(a, b):
    return lax.dot_general(a, b, (((1,), (1,)), ((), ())), preferred_element_type=jnp.float32)


def shard_cols(shard):
    return pl.ds(pl.multiple_of(shard * ROWS, 128), ROWS)


def scale_by_gain(value, gain, shard):
    parts = []
    for part in range(ROWS // 128):
        row = gain[pl.ds(shard * (ROWS // 128) + part, 1), :]
        parts.append(value[:, part * 128:(part + 1) * 128] * row)
    return jnp.concatenate(parts, axis=1)


def half(zh, c, mine, theirs, x, kg, gain, weights, scaled):
    total = dot(mine[:, shard_cols(zh)], weights[0][...]) + dot(theirs[:, shard_cols(zh)], weights[1][...])
    inner = jnp.zeros((T, 1), jnp.float32)
    for k, shard in enumerate((2 * zh + c, 2 * zh + 1 - c)):
        value = scale_by_gain(dot_t(kg[...], weights[k][...]), gain, shard)
        scaled[:, k * ROWS:(k + 1) * ROWS] = value
        inner += jnp.sum(value * x[:, shard_cols(shard)].astype(jnp.float32), axis=1, keepdims=True)
    return total, inner


def near_kernel(where, mine, theirs, x, kg, gain, own, other, keys, inner, scaled):
    c, zh, _, _ = unpack(where)
    keys[...], inner[...] = half(zh, c, mine, theirs, x, kg, gain, (own, other), scaled)


def near_call(where, mine, theirs, tokens, key_grad, gain, own, other):
    return pl.pallas_call(
        near_kernel,
        in_specs=[pl.BlockSpec(memory_space=pltpu.SMEM)] + vmem(7),
        out_specs=vmem(3),
        out_shape=[
            jax.ShapeDtypeStruct((T, KH), jnp.float32),
            jax.ShapeDtypeStruct((T, 1), jnp.float32),
            jax.ShapeDtypeStruct((T, D // 2), jnp.float32),
        ],
        cost_estimate=pl.CostEstimate(flops=2 * T * D * KH, bytes_accessed=18 << 20, transcendentals=0),
        compiler_params=pltpu.CompilerParams(vmem_limit_bytes=12 << 20),
        name="near",
    )(where, mine, theirs, tokens, key_grad, gain, own, other)


def keys_kernel(where, mine, theirs, near, far, far_other, out):
    there = shard_cols(1 - unpack(where)[1])
    total = near[...] + dot(mine[:, there], far[...]) + dot(theirs[:, there], far_other[...])
    out[...] = total.astype(jnp.bfloat16)


def keys_call(where, mine, theirs, near, far, far_other):
    return pl.pallas_call(
        keys_kernel,
        in_specs=[pl.BlockSpec(memory_space=pltpu.SMEM)] + vmem(5),
        out_specs=vmem(1)[0],
        out_shape=jax.ShapeDtypeStruct((T, KH), jnp.bfloat16),
        cost_estimate=pl.CostEstimate(flops=T * D * KH, bytes_accessed=10 << 20, transcendentals=0),
        compiler_params=pltpu.CompilerParams(vmem_limit_bytes=6 << 20),
        name="keys",
    )(where, mine, theirs, near, far, far_other)


def back_kernel(where, x, kg, inv_ref, gain, inner_ref, scaled, far, far_other, out, hold):
    c, zh, _, _ = unpack(where)
    inner = inner_ref[...]
    shards = (2 * (1 - zh) + c, 2 * (1 - zh) + 1 - c)
    for k, (shard, weight) in enumerate(zip(shards, (far, far_other))):
        value = scale_by_gain(dot_t(kg[...], weight[...]), gain, shard)
        hold[:, k * ROWS:(k + 1) * ROWS] = value
        inner += jnp.sum(value * x[:, shard_cols(shard)].astype(jnp.float32), axis=1, keepdims=True)
    inv = inv_ref[...]
    pull = inv * inv * inv * (inner * (1.0 / D))
    for source, shards in ((scaled, (2 * zh + c, 2 * zh + 1 - c)), (hold, shards)):
        for k, shard in enumerate(shards):
            xf = x[:, shard_cols(shard)].astype(jnp.float32)
            value = inv * source[:, k * ROWS:(k + 1) * ROWS] - xf * pull
            out[:, shard_cols(shard)] = value.astype(jnp.bfloat16)


def back_call(where, tokens, key_grad, inv, gain, inner, scaled, far, far_other):
    return pl.pallas_call(
        back_kernel,
        in_specs=[pl.BlockSpec(memory_space=pltpu.SMEM)] + vmem(8),
        out_specs=vmem(1)[0],
        out_shape=jax.ShapeDtypeStruct((T, D), jnp.bfloat16),
        scratch_shapes=[pltpu.VMEM((T, D // 2), jnp.float32)],
        cost_estimate=pl.CostEstimate(flops=T * D * KH, bytes_accessed=16 << 20, transcendentals=0),
        compiler_params=pltpu.CompilerParams(vmem_limit_bytes=14 << 20),
        name="back",
    )(where, tokens, key_grad, inv, gain, inner, scaled, far, far_other)


def device_step(tokens, gain, key_grad, weight, m_code, m_exp, v_code, v_exp):
    zh, c = lax.axis_index("zh"), lax.axis_index("c")
    y, x = lax.axis_index("y"), lax.axis_index("x")
    pos = jnp.where(c == 0, x, y)
    pos_other = jnp.where(c == 0, y, x)
    where = (c + 2 * zh + 4 * pos + 16 * pos_other).astype(jnp.int32).reshape(1)

    gain = gain.reshape(D // 128, 128)

    far = send(weight, across)
    kg_other = send(key_grad, partner)
    w_other = send(weight, partner)

    theirs, inv, tokens, gain = norm_call(where, tokens, gain)
    received = send(theirs, partner)
    mine, mine_t = mine_call(where, tokens, inv, gain)
    received_t, part2 = grad_call((2,), where, mine_t, received, key_grad, kg_other, first=True)
    part2 = send(part2, around(2))
    part1, part3 = grad_call((1, 3), where, mine_t, received_t, key_grad, kg_other)
    part1, part3 = send(part1, around(1)), send(part3, around(3))
    part0, = grad_call((0,), where, mine_t, received_t, key_grad, kg_other, dtype=jnp.float32)
    parts = [part0, part1, part3, part2]
    near_keys, inner, scaled = near_call(where, mine, theirs, tokens, key_grad, gain, weight, w_other)
    old = old_call(m_exp, v_exp, m_code, v_code)
    parts = list(first_sum(parts))
    far_other = send(far, partner)
    parts = [parts[0]] + [send(parts[k], around(k, True)) for k in RING[1:]]
    keys = keys_call(where, mine, theirs, near_keys, far, far_other)
    keep, give = second_sum(where, parts)
    near = send(keep, zl_partner)
    across_z = send(give, across)
    opposite_z = send(give, opposite)
    total = total_call(keep, near, across_z, opposite_z)

    total = join_call([total] + send_ring(total, True))
    got = send_ring(total, False)
    *done, scales = adam_own(where, total, old)
    token_grad = back_call(where, tokens, key_grad, inv, gain, inner, scaled, far, far_other)
    outs = adam_more(RING[1:], True, where, got, old, scales, done)
    step, m_rel, v_rel, m_scale, v_scale = outs
    return keys, token_grad, step, m_rel, m_scale.T, v_rel, v_scale.T


def solution(mesh):
    inner = Mesh(mesh.devices.reshape(2, 2, 4, 4, 2), AXES)
    tok = P(AXES, None)
    row = P(("zh", "c"), None)

    return jax.shard_map(
        device_step,
        mesh=inner,
        in_specs=(tok, P(None), tok, row, row, row, row, row),
        out_specs=(tok, tok, row, row, row, row, row),
        check_vma=False,
    )
```

```python
import functools

import jax
import jax.numpy as jnp
from jax import lax
from jax.experimental import pallas as pl
from jax.experimental.pallas import tpu as pltpu
from jax.sharding import Mesh, PartitionSpec as P


bias_first = 0.9999734386011124
bias_second = 0.0952078528862904

AXES = ("zh", "c", "y", "x", "zl")

D = 4608
KH = 1024
ROWS = 1152
T = 384
RING = (0, 1, 3, 2)
RB, CB = 144, 256


def index_of(zh, c, y, x, zl):
    return (((zh * 2 + c) * 4 + y) * 4 + x) * 2 + zl


def pairs(move):
    out = []
    for zh in range(2):
        for c in range(2):
            for y in range(4):
                for x in range(4):
                    for zl in range(2):
                        to = move(zh, c, y, x, zl)
                        out.append((index_of(zh, c, y, x, zl), index_of(*to)))
    return out


def partner(zh, c, y, x, zl):
    return zh, 1 - c, y, x, zl


def across(zh, c, y, x, zl):
    return 1 - zh, c, y, x, 1 - zl


def zl_partner(zh, c, y, x, zl):
    return zh, c, y, x, 1 - zl


def opposite(zh, c, y, x, zl):
    return 1 - zh, c, y, x, zl


def around(step, second=False):
    def move(zh, c, y, x, zl):
        if (c == 0) != second:
            return zh, c, y, (x + step) % 4, zl
        return zh, c, (y + step) % 4, x, zl

    return move


def send(value, move):
    return lax.ppermute(value, AXES, pairs(move))


def send_ring(value, second):
    return [send(value, around(k, second)) for k in RING[1:]]


def unpack(where):
    w = where[0]
    return w % 2, (w // 2) % 2, (w // 4) % 4, w // 16


def vmem(n):
    return [pl.BlockSpec(memory_space=pltpu.VMEM)] * n


STEP = 64


def norm_columns(x, inv, gain, core, rows, out):
    for half in range(2):
        for part in range(ROWS // 128):
            at = (half * 2 + core) * (ROWS // 128) + part
            cols = pl.ds(pl.multiple_of(at * 128, 128), 128)
            value = x[rows, cols].astype(jnp.float32) * inv[rows, :] * gain[pl.ds(at, 1), :]
            out[rows, half * ROWS + part * 128:half * ROWS + (part + 1) * 128] = value.astype(jnp.bfloat16)


def norm_kernel(where, x_hbm, gain_hbm, theirs, inv, x, gain, sems):
    rows = [slice(k * STEP, (k + 1) * STEP) for k in range(T // STEP)]
    copies = [pltpu.make_async_copy(x_hbm.at[r], x.at[r], sems.at[k]) for k, r in enumerate(rows)]
    gain_copy = pltpu.make_async_copy(gain_hbm, gain, sems.at[len(rows)])
    gain_copy.start()
    for copy in copies:
        copy.start()
    gain_copy.wait()
    c = unpack(where)[0]
    for copy, r in zip(copies, rows):
        copy.wait()
        xf = x[r, :].astype(jnp.float32)
        inv[r, :] = lax.rsqrt(jnp.mean(xf * xf, axis=1, keepdims=True) + 1e-06)
        norm_columns(x, inv, gain, 1 - c, r, theirs)


def norm_call(where, tokens, gain):
    return pl.pallas_call(
        norm_kernel,
        in_specs=[pl.BlockSpec(memory_space=pltpu.SMEM)] + [pl.BlockSpec(memory_space=pltpu.HBM)] * 2,
        out_specs=vmem(4),
        out_shape=[
            jax.ShapeDtypeStruct((T, D // 2), jnp.bfloat16),
            jax.ShapeDtypeStruct((T, 1), jnp.float32),
            jax.ShapeDtypeStruct((T, D), jnp.bfloat16),
            jax.ShapeDtypeStruct((D // 128, 128), jnp.float32),
        ],
        scratch_shapes=[pltpu.SemaphoreType.DMA((T // STEP + 1,))],
        cost_estimate=pl.CostEstimate(flops=4 * T * D, bytes_accessed=4 * T * D, transcendentals=T),
        compiler_params=pltpu.CompilerParams(vmem_limit_bytes=8 << 20),
        name="norm",
    )(where, *(pltpu.with_memory_space_constraint(v, pltpu.HBM) for v in (tokens, gain)))


def flip(in_ref, out_ref):
    for part in range(D // 2 // 128):
        cols = slice(part * 128, (part + 1) * 128)
        out_ref[cols, :] = in_ref[:, cols].T


def mine_kernel(where, x, inv, gain, mine, mine_t):
    for k in range(T // STEP):
        norm_columns(x, inv, gain, unpack(where)[0], slice(k * STEP, (k + 1) * STEP), mine)
    flip(mine, mine_t)


def mine_call(where, tokens, inv, gain):
    return pl.pallas_call(
        mine_kernel,
        in_specs=[pl.BlockSpec(memory_space=pltpu.SMEM)] + vmem(3),
        out_specs=vmem(2),
        out_shape=[
            jax.ShapeDtypeStruct((T, D // 2), jnp.bfloat16),
            jax.ShapeDtypeStruct((D // 2, T), jnp.bfloat16),
        ],
        cost_estimate=pl.CostEstimate(flops=2 * T * D, bytes_accessed=3 * T * D, transcendentals=0),
        compiler_params=pltpu.CompilerParams(vmem_limit_bytes=6 << 20),
        name="mine",
    )(where, tokens, inv, gain)


def grad_columns(where, a_ref, b_ref, ka_ref, kb_ref, k, out):
    _, _, pos, other = unpack(where)
    cols = pl.ds(pl.multiple_of(lax.rem(pos + k, 4) * CB, 128), CB)
    for zh in range(2):
        rows = slice(zh * ROWS, (zh + 1) * ROWS)
        acc = dot(a_ref[rows, :], ka_ref[:, cols]) + dot(b_ref[rows, :], kb_ref[:, cols])
        for o in range(4):
            for zl in range(2):
                at = (o * 2 + zl) * RB
                out[lax.rem(o + 4 - other, 4), zh, zl] = acc[at:at + RB, :].astype(out.dtype)


def first_grad_kernel(where, a_ref, b_in, ka_ref, kb_ref, b_ref, out):
    flip(b_in, b_ref)
    grad_columns(where, a_ref, b_ref, ka_ref, kb_ref, 2, out)


def grad_kernel(ks, where, *refs):
    for k, out in zip(ks, refs[4:]):
        grad_columns(where, *refs[:4], k, out)


def grad_call(ks, where, a, b, ka, kb, dtype=jnp.bfloat16, first=False):
    out = [jax.ShapeDtypeStruct((4, 2, 2, RB, CB), dtype)] * len(ks)
    return pl.pallas_call(
        first_grad_kernel if first else functools.partial(grad_kernel, ks),
        in_specs=[pl.BlockSpec(memory_space=pltpu.SMEM)] + vmem(4),
        out_specs=vmem(len(ks) + first),
        out_shape=[jax.ShapeDtypeStruct((D // 2, T), jnp.bfloat16)] * first + out,
        cost_estimate=pl.CostEstimate(flops=T * D * KH // 2 * len(ks), bytes_accessed=6 << 20, transcendentals=0),
        compiler_params=pltpu.CompilerParams(vmem_limit_bytes=8 << 20),
        name="grad",
    )(where, a, b, ka, kb)


def add_up(refs):
    total = refs[0][...].astype(jnp.float32)
    for ref in refs[1:]:
        total += ref[...].astype(jnp.float32)
    return total


def first_sum_kernel(*refs):
    for j in range(4):
        refs[4 + j][...] = add_up([ref.at[j] for ref in refs[:4]]).astype(refs[4 + j].dtype)


def first_sum(parts):
    return pl.pallas_call(
        first_sum_kernel,
        in_specs=vmem(4),
        out_specs=vmem(4),
        out_shape=[jax.ShapeDtypeStruct((2, 2, RB, CB), kind) for kind in (jnp.float32,) + (jnp.bfloat16,) * 3],
        cost_estimate=pl.CostEstimate(flops=64 * RB * CB, bytes_accessed=6 << 20, transcendentals=0),
        compiler_params=pltpu.CompilerParams(vmem_limit_bytes=8 << 20),
        name="first_sum",
    )(*parts)


def second_sum_kernel(where, *refs):
    zh = unpack(where)[1]
    for out, h in ((refs[4], zh), (refs[5], 1 - zh)):
        out[...] = add_up([ref.at[h] for ref in refs[:4]]).astype(jnp.bfloat16)


def second_sum(where, parts):
    return pl.pallas_call(
        second_sum_kernel,
        in_specs=[pl.BlockSpec(memory_space=pltpu.SMEM)] + vmem(4),
        out_specs=vmem(2),
        out_shape=[jax.ShapeDtypeStruct((2, RB, CB), jnp.bfloat16)] * 2,
        cost_estimate=pl.CostEstimate(flops=16 * RB * CB, bytes_accessed=2 << 20, transcendentals=0),
        compiler_params=pltpu.CompilerParams(vmem_limit_bytes=4 << 20),
        name="second_sum",
    )(where, *parts)


def total_kernel(own, near, across_z, far, out):
    near_sum = own[...].astype(jnp.float32) + near[...].astype(jnp.float32)
    far_sum = across_z[...].astype(jnp.float32) + far[...].astype(jnp.float32)
    out[...] = (near_sum + far_sum).astype(jnp.bfloat16)


def total_call(*parts):
    return pl.pallas_call(
        total_kernel,
        in_specs=vmem(4),
        out_specs=vmem(1)[0],
        out_shape=jax.ShapeDtypeStruct((2, RB, CB), jnp.bfloat16),
        cost_estimate=pl.CostEstimate(flops=8 * RB * CB, bytes_accessed=1 << 20, transcendentals=0),
        compiler_params=pltpu.CompilerParams(vmem_limit_bytes=4 << 20),
        name="total",
    )(*parts)


def join_kernel(*refs):
    for k, ref in zip(RING, refs[:4]):
        refs[4][k] = ref[...]


def join_call(parts):
    return pl.pallas_call(
        join_kernel,
        in_specs=vmem(4),
        out_specs=vmem(1)[0],
        out_shape=jax.ShapeDtypeStruct((4, 2, RB, CB), jnp.bfloat16),
        cost_estimate=pl.CostEstimate(flops=0, bytes_accessed=1 << 20, transcendentals=0),
        compiler_params=pltpu.CompilerParams(vmem_limit_bytes=4 << 20),
        name="join",
    )(*parts)


SCALE = bias_first * bias_first / bias_second


def old_kernel(me_ref, ve_ref, mc_ref, vc_ref, m_ref, w_ref, hold):
    hold[...] = jnp.zeros_like(hold)
    for part in range(ROWS // 128):
        rows = slice(part * 128, (part + 1) * 128)
        hold[0:4, :] = jnp.exp2(me_ref[:, rows].astype(jnp.float32)) * (0.9 / 127.0)
        hold[4:8, :] = jnp.exp2(ve_ref[:, rows].astype(jnp.float32)) * (0.999 * SCALE / 255.0)
        unit = hold[...].T
        for cb in range(4):
            cols = slice(cb * CB, (cb + 1) * CB)
            m_ref[rows, cols] = mc_ref[rows, cols].astype(jnp.float32) * unit[:, cb:cb + 1]
            w_ref[rows, cols] = vc_ref[rows, cols].astype(jnp.float32) * unit[:, 4 + cb:5 + cb]


def old_call(m_exp, v_exp, m_code, v_code):
    return pl.pallas_call(
        old_kernel,
        in_specs=vmem(4),
        out_specs=vmem(2),
        out_shape=[jax.ShapeDtypeStruct((ROWS, KH), jnp.float32)] * 2,
        scratch_shapes=[pltpu.VMEM((128, 128), jnp.float32)],
        cost_estimate=pl.CostEstimate(flops=4 * ROWS * KH, bytes_accessed=14 << 20, transcendentals=8 * ROWS),
        compiler_params=pltpu.CompilerParams(vmem_limit_bytes=12 << 20),
        name="old",
    )(m_exp.T, v_exp.T, m_code, v_code)


def adam_rows(other, half, read, m_old, w_old, step_ref, mr_ref, vr_ref, keep_scale):
    lane = lax.broadcasted_iota(jnp.int32, (RB, 128), 1)
    for b in range(4):
        rows = slice(b * RB, (b + 1) * RB)
        back = lax.rem(other + 8 - (2 * half + b // 2), 4)
        g = read(back, b % 2).astype(jnp.float32)
        m = m_old[rows, :] + 0.1 * g
        w = w_old[rows, :] + (0.001 * SCALE) * (g * g)
        step_ref[rows, :] = m / (w * lax.rsqrt(w) + 1e-08 * bias_first)
        ms = jnp.max(jnp.abs(m), axis=1, keepdims=True)
        vs = jnp.max(w, axis=1, keepdims=True) * (1.0 / SCALE)
        keep_scale(b, lane, ms, vs)
        mr_ref[rows, :] = (m * (1.0 / (ms + 1e-06))).astype(jnp.bfloat16)
        vr_ref[rows, :] = (w * ((1.0 / SCALE) / (vs + 1e-06))).astype(jnp.bfloat16)


def adam_own_kernel(where, g_ref, m_old, w_old, step_ref, mr_ref, vr_ref, scale_ref):
    _, _, p, other = unpack(where)

    def keep_scale(b, lane, ms, vs):
        scale_ref[b * RB:(b + 1) * RB, :] = jnp.where(lane == p, ms, jnp.where(lane == 4 + p, vs, 0.0))

    adam_rows(
        other, pl.program_id(0), lambda back, zl: g_ref[back, zl],
        m_old, w_old, step_ref, mr_ref, vr_ref, keep_scale,
    )


WIDE = [
    jax.ShapeDtypeStruct((ROWS, KH), jnp.float32),
    jax.ShapeDtypeStruct((ROWS, KH), jnp.bfloat16),
    jax.ShapeDtypeStruct((ROWS, KH), jnp.bfloat16),
]


def adam_own(where, g, old):
    wide = pl.BlockSpec((4 * RB, CB), lambda i, where: (i, (where[0] // 4) % 4))
    thin = pl.BlockSpec((4 * RB, 128), lambda i, where: (i, 0))
    return pl.pallas_call(
        adam_own_kernel,
        grid_spec=pltpu.PrefetchScalarGridSpec(
            num_scalar_prefetch=1,
            grid=(2,),
            in_specs=[pl.BlockSpec((4, 2, RB, CB), lambda i, where: (0, 0, 0, 0)), wide, wide],
            out_specs=[wide, wide, wide, thin],
        ),
        out_shape=WIDE + [jax.ShapeDtypeStruct((ROWS, 128), jnp.float32)],
        cost_estimate=pl.CostEstimate(flops=5 * ROWS * KH, bytes_accessed=4 << 20, transcendentals=ROWS * KH // 2),
        compiler_params=pltpu.CompilerParams(vmem_limit_bytes=10 << 20),
        name="adam_own",
    )(where, g, *old)


def place_of(ks, i, pos):
    k = ks[0]
    for n in range(1, len(ks)):
        k = jnp.where(i < 2 * n, k, ks[n])
    return lax.rem(pos + 4 - k, 4)


def adam_more_kernel(ks, last, where, *refs):
    n = len(ks)
    gs, (m_old, w_old, s0) = refs[:n], refs[n:n + 3]
    step_ref, mr_ref, vr_ref = refs[n + 6:n + 9]
    scales = refs[-1]
    _, _, pos, other = unpack(where)
    i = pl.program_id(0)
    p, half = place_of(ks, i, pos), lax.rem(i, 2)

    @pl.when(i == 0)
    def _():
        scales[...] = s0[...]

    def keep_scale(b, lane, ms, vs):
        rows = pl.ds(pl.multiple_of(half * (4 * RB) + b * RB, 8), RB)
        scales[rows, :] = jnp.where(lane == p, ms, jnp.where(lane == 4 + p, vs, scales[rows, :]))

    def read(back, zl):
        g = gs[0][back, zl]
        for k in range(1, n):
            g = jnp.where(i < 2 * k, g, gs[k][back, zl])
        return g

    adam_rows(other, half, read, m_old, w_old, step_ref, mr_ref, vr_ref, keep_scale)

    if last:
        @pl.when(i == 2 * n - 1)
        def _():
            for part in range(ROWS // 128):
                cols = slice(part * 128, (part + 1) * 128)
                turned = scales[cols, :].T
                refs[n + 9][:, cols] = turned[0:4, :]
                refs[n + 10][:, cols] = turned[4:8, :]


def adam_more(ks, last, where, g, old, s0, done):
    n = len(ks)
    wide = pl.BlockSpec((4 * RB, CB), lambda i, where: (lax.rem(i, 2), place_of(ks, i, (where[0] // 4) % 4)))
    flat = pl.BlockSpec((4, ROWS), lambda i, where: (0, 0))
    tall = pl.BlockSpec((ROWS, 128), lambda i, where: (0, 0))
    whole = pl.BlockSpec((4, 2, RB, CB), lambda i, where: (0, 0, 0, 0))
    scale_shapes = [jax.ShapeDtypeStruct((4, ROWS), jnp.float32)] * 2 if last else [jax.ShapeDtypeStruct((ROWS, 128), jnp.float32)]
    return pl.pallas_call(
        functools.partial(adam_more_kernel, ks, last),
        grid_spec=pltpu.PrefetchScalarGridSpec(
            num_scalar_prefetch=1,
            grid=(2 * n,),
            in_specs=[whole] * n + [wide, wide, tall] + [pl.BlockSpec(memory_space=pl.ANY)] * 3,
            out_specs=[wide, wide, wide] + ([flat, flat] if last else [tall]),
            scratch_shapes=[pltpu.VMEM((ROWS, 128), jnp.float32)] * last,
        ),
        out_shape=WIDE + scale_shapes,
        input_output_aliases={n + 4: 0, n + 5: 1, n + 6: 2},
        cost_estimate=pl.CostEstimate(flops=5 * n * ROWS * KH, bytes_accessed=n * (4 << 20), transcendentals=n * ROWS * KH // 2),
        compiler_params=pltpu.CompilerParams(vmem_limit_bytes=12 << 20),
        name="adam_more",
    )(where, *g, *old, s0, *done)


def dot(a, b):
    return jnp.dot(a, b, preferred_element_type=jnp.float32)


def dot_t(a, b):
    return lax.dot_general(a, b, (((1,), (1,)), ((), ())), preferred_element_type=jnp.float32)


def shard_cols(shard):
    return pl.ds(pl.multiple_of(shard * ROWS, 128), ROWS)


def scale_by_gain(value, gain, shard):
    parts = []
    for part in range(ROWS // 128):
        row = gain[pl.ds(shard * (ROWS // 128) + part, 1), :]
        parts.append(value[:, part * 128:(part + 1) * 128] * row)
    return jnp.concatenate(parts, axis=1)


def half(zh, c, mine, theirs, x, kg, gain, weights, scaled):
    total = dot(mine[:, shard_cols(zh)], weights[0][...]) + dot(theirs[:, shard_cols(zh)], weights[1][...])
    inner = jnp.zeros((T, 1), jnp.float32)
    for k, shard in enumerate((2 * zh + c, 2 * zh + 1 - c)):
        value = scale_by_gain(dot_t(kg[...], weights[k][...]), gain, shard)
        scaled[:, k * ROWS:(k + 1) * ROWS] = value
        inner += jnp.sum(value * x[:, shard_cols(shard)].astype(jnp.float32), axis=1, keepdims=True)
    return total, inner


def near_kernel(where, mine, theirs, x, kg, gain, own, other, keys, inner, scaled):
    c, zh, _, _ = unpack(where)
    keys[...], inner[...] = half(zh, c, mine, theirs, x, kg, gain, (own, other), scaled)


def near_call(where, mine, theirs, tokens, key_grad, gain, own, other):
    return pl.pallas_call(
        near_kernel,
        in_specs=[pl.BlockSpec(memory_space=pltpu.SMEM)] + vmem(7),
        out_specs=vmem(3),
        out_shape=[
            jax.ShapeDtypeStruct((T, KH), jnp.float32),
            jax.ShapeDtypeStruct((T, 1), jnp.float32),
            jax.ShapeDtypeStruct((T, D // 2), jnp.float32),
        ],
        cost_estimate=pl.CostEstimate(flops=2 * T * D * KH, bytes_accessed=18 << 20, transcendentals=0),
        compiler_params=pltpu.CompilerParams(vmem_limit_bytes=12 << 20),
        name="near",
    )(where, mine, theirs, tokens, key_grad, gain, own, other)


def keys_kernel(where, mine, theirs, near, far, far_other, out):
    there = shard_cols(1 - unpack(where)[1])
    total = near[...] + dot(mine[:, there], far[...]) + dot(theirs[:, there], far_other[...])
    out[...] = total.astype(jnp.bfloat16)


def keys_call(where, mine, theirs, near, far, far_other):
    return pl.pallas_call(
        keys_kernel,
        in_specs=[pl.BlockSpec(memory_space=pltpu.SMEM)] + vmem(5),
        out_specs=vmem(1)[0],
        out_shape=jax.ShapeDtypeStruct((T, KH), jnp.bfloat16),
        cost_estimate=pl.CostEstimate(flops=T * D * KH, bytes_accessed=10 << 20, transcendentals=0),
        compiler_params=pltpu.CompilerParams(vmem_limit_bytes=6 << 20),
        name="keys",
    )(where, mine, theirs, near, far, far_other)


def back_kernel(where, x, kg, inv_ref, gain, inner_ref, scaled, far, far_other, out, hold):
    c, zh, _, _ = unpack(where)
    inner = inner_ref[...]
    shards = (2 * (1 - zh) + c, 2 * (1 - zh) + 1 - c)
    for k, (shard, weight) in enumerate(zip(shards, (far, far_other))):
        value = scale_by_gain(dot_t(kg[...], weight[...]), gain, shard)
        hold[:, k * ROWS:(k + 1) * ROWS] = value
        inner += jnp.sum(value * x[:, shard_cols(shard)].astype(jnp.float32), axis=1, keepdims=True)
    inv = inv_ref[...]
    pull = inv * inv * inv * (inner * (1.0 / D))
    for source, shards in ((scaled, (2 * zh + c, 2 * zh + 1 - c)), (hold, shards)):
        for k, shard in enumerate(shards):
            xf = x[:, shard_cols(shard)].astype(jnp.float32)
            value = inv * source[:, k * ROWS:(k + 1) * ROWS] - xf * pull
            out[:, shard_cols(shard)] = value.astype(jnp.bfloat16)


def back_call(where, tokens, key_grad, inv, gain, inner, scaled, far, far_other):
    return pl.pallas_call(
        back_kernel,
        in_specs=[pl.BlockSpec(memory_space=pltpu.SMEM)] + vmem(8),
        out_specs=vmem(1)[0],
        out_shape=jax.ShapeDtypeStruct((T, D), jnp.bfloat16),
        scratch_shapes=[pltpu.VMEM((T, D // 2), jnp.float32)],
        cost_estimate=pl.CostEstimate(flops=T * D * KH, bytes_accessed=16 << 20, transcendentals=0),
        compiler_params=pltpu.CompilerParams(vmem_limit_bytes=14 << 20),
        name="back",
    )(where, tokens, key_grad, inv, gain, inner, scaled, far, far_other)


def device_step(tokens, gain, key_grad, weight, m_code, m_exp, v_code, v_exp):
    zh, c = lax.axis_index("zh"), lax.axis_index("c")
    y, x = lax.axis_index("y"), lax.axis_index("x")
    pos = jnp.where(c == 0, x, y)
    pos_other = jnp.where(c == 0, y, x)
    where = (c + 2 * zh + 4 * pos + 16 * pos_other).astype(jnp.int32).reshape(1)

    gain = gain.reshape(D // 128, 128)

    far = send(weight, across)
    kg_other = send(key_grad, partner)
    w_other = send(weight, partner)

    theirs, inv, tokens, gain = norm_call(where, tokens, gain)
    received = send(theirs, partner)
    mine, mine_t = mine_call(where, tokens, inv, gain)
    received_t, part2 = grad_call((2,), where, mine_t, received, key_grad, kg_other, first=True)
    part2 = send(part2, around(2))
    part1, part3 = grad_call((1, 3), where, mine_t, received_t, key_grad, kg_other)
    part1, part3 = send(part1, around(1)), send(part3, around(3))
    part0, = grad_call((0,), where, mine_t, received_t, key_grad, kg_other, dtype=jnp.float32)
    parts = [part0, part1, part3, part2]
    near_keys, inner, scaled = near_call(where, mine, theirs, tokens, key_grad, gain, weight, w_other)
    old = old_call(m_exp, v_exp, m_code, v_code)
    parts = list(first_sum(parts))
    far_other = send(far, partner)
    parts = [parts[0]] + [send(parts[k], around(k, True)) for k in RING[1:]]
    keys = keys_call(where, mine, theirs, near_keys, far, far_other)
    keep, give = second_sum(where, parts)
    near = send(keep, zl_partner)
    across_z = send(give, across)
    opposite_z = send(give, opposite)
    total = total_call(keep, near, across_z, opposite_z)

    total = join_call([total] + send_ring(total, True))
    got = send_ring(total, False)
    *done, scales = adam_own(where, total, old)
    token_grad = back_call(where, tokens, key_grad, inv, gain, inner, scaled, far, far_other)
    outs = adam_more(RING[1:], True, where, got, old, scales, done)
    step, m_rel, v_rel, m_scale, v_scale = outs
    return keys, token_grad, step, m_rel, m_scale.T, v_rel, v_scale.T


def solution(mesh):
    inner = Mesh(mesh.devices.reshape(2, 2, 4, 4, 2), AXES)
    tok = P(AXES, None)
    row = P(("zh", "c"), None)

    return jax.shard_map(
        device_step,
        mesh=inner,
        in_specs=(tok, P(None), tok, row, row, row, row, row),
        out_specs=(tok, tok, row, row, row, row, row),
        check_vma=False,
    )
```

```python
import functools

import jax
import jax.numpy as jnp
from jax import lax
from jax.experimental import pallas as pl
from jax.experimental.pallas import tpu as pltpu
from jax.sharding import Mesh, PartitionSpec as P


bias_first = 0.9999734386011124
bias_second = 0.0952078528862904

AXES = ("zh", "c", "y", "x", "zl")

D = 4608
KH = 1024
ROWS = 1152
T = 384
RING = (0, 1, 3, 2)
RB, CB = 144, 256


def index_of(zh, c, y, x, zl):
    return (((zh * 2 + c) * 4 + y) * 4 + x) * 2 + zl


def pairs(move):
    out = []
    for zh in range(2):
        for c in range(2):
            for y in range(4):
                for x in range(4):
                    for zl in range(2):
                        to = move(zh, c, y, x, zl)
                        out.append((index_of(zh, c, y, x, zl), index_of(*to)))
    return out


def partner(zh, c, y, x, zl):
    return zh, 1 - c, y, x, zl


def across(zh, c, y, x, zl):
    return 1 - zh, c, y, x, 1 - zl


def zl_partner(zh, c, y, x, zl):
    return zh, c, y, x, 1 - zl


def opposite(zh, c, y, x, zl):
    return 1 - zh, c, y, x, zl


def around(step, second=False):
    def move(zh, c, y, x, zl):
        if (c == 0) != second:
            return zh, c, y, (x + step) % 4, zl
        return zh, c, (y + step) % 4, x, zl

    return move


def send(value, move):
    return lax.ppermute(value, AXES, pairs(move))


def send_ring(value, second):
    return [send(value, around(k, second)) for k in RING[1:]]


def unpack(where):
    w = where[0]
    return w % 2, (w // 2) % 2, (w // 4) % 4, w // 16


def vmem(n):
    return [pl.BlockSpec(memory_space=pltpu.VMEM)] * n


STEP = 64


def norm_columns(x, inv, gain, core, rows, out):
    for half in range(2):
        for part in range(ROWS // 128):
            at = (half * 2 + core) * (ROWS // 128) + part
            cols = pl.ds(pl.multiple_of(at * 128, 128), 128)
            value = x[rows, cols].astype(jnp.float32) * inv[rows, :] * gain[pl.ds(at, 1), :]
            out[rows, half * ROWS + part * 128:half * ROWS + (part + 1) * 128] = value.astype(jnp.bfloat16)


def norm_kernel(where, x_hbm, gain_hbm, theirs, inv, x, gain, sems):
    rows = [slice(k * STEP, (k + 1) * STEP) for k in range(T // STEP)]
    copies = [pltpu.make_async_copy(x_hbm.at[r], x.at[r], sems.at[k]) for k, r in enumerate(rows)]
    gain_copy = pltpu.make_async_copy(gain_hbm, gain, sems.at[len(rows)])
    gain_copy.start()
    for copy in copies:
        copy.start()
    gain_copy.wait()
    c = unpack(where)[0]
    for copy, r in zip(copies, rows):
        copy.wait()
        xf = x[r, :].astype(jnp.float32)
        inv[r, :] = lax.rsqrt(jnp.mean(xf * xf, axis=1, keepdims=True) + 1e-06)
        norm_columns(x, inv, gain, 1 - c, r, theirs)


def norm_call(where, tokens, gain):
    return pl.pallas_call(
        norm_kernel,
        in_specs=[pl.BlockSpec(memory_space=pltpu.SMEM)] + [pl.BlockSpec(memory_space=pltpu.HBM)] * 2,
        out_specs=vmem(4),
        out_shape=[
            jax.ShapeDtypeStruct((T, D // 2), jnp.bfloat16),
            jax.ShapeDtypeStruct((T, 1), jnp.float32),
            jax.ShapeDtypeStruct((T, D), jnp.bfloat16),
            jax.ShapeDtypeStruct((D // 128, 128), jnp.float32),
        ],
        scratch_shapes=[pltpu.SemaphoreType.DMA((T // STEP + 1,))],
        cost_estimate=pl.CostEstimate(flops=4 * T * D, bytes_accessed=4 * T * D, transcendentals=T),
        compiler_params=pltpu.CompilerParams(vmem_limit_bytes=8 << 20),
        name="norm",
    )(where, *(pltpu.with_memory_space_constraint(v, pltpu.HBM) for v in (tokens, gain)))


def flip(in_ref, out_ref):
    for part in range(D // 2 // 128):
        cols = slice(part * 128, (part + 1) * 128)
        out_ref[cols, :] = in_ref[:, cols].T


def mine_kernel(where, x, inv, gain, mine, mine_t):
    for k in range(T // STEP):
        norm_columns(x, inv, gain, unpack(where)[0], slice(k * STEP, (k + 1) * STEP), mine)
    flip(mine, mine_t)


def mine_call(where, tokens, inv, gain):
    return pl.pallas_call(
        mine_kernel,
        in_specs=[pl.BlockSpec(memory_space=pltpu.SMEM)] + vmem(3),
        out_specs=vmem(2),
        out_shape=[
            jax.ShapeDtypeStruct((T, D // 2), jnp.bfloat16),
            jax.ShapeDtypeStruct((D // 2, T), jnp.bfloat16),
        ],
        cost_estimate=pl.CostEstimate(flops=2 * T * D, bytes_accessed=3 * T * D, transcendentals=0),
        compiler_params=pltpu.CompilerParams(vmem_limit_bytes=6 << 20),
        name="mine",
    )(where, tokens, inv, gain)


def grad_columns(where, a_ref, b_ref, ka_ref, kb_ref, k, out):
    _, _, pos, other = unpack(where)
    cols = pl.ds(pl.multiple_of(lax.rem(pos + k, 4) * CB, 128), CB)
    for zh in range(2):
        rows = slice(zh * ROWS, (zh + 1) * ROWS)
        acc = dot(a_ref[rows, :], ka_ref[:, cols]) + dot(b_ref[rows, :], kb_ref[:, cols])
        for o in range(4):
            for zl in range(2):
                at = (o * 2 + zl) * RB
                out[lax.rem(o + 4 - other, 4), zh, zl] = acc[at:at + RB, :].astype(out.dtype)


def first_grad_kernel(where, a_ref, b_in, ka_ref, kb_ref, b_ref, out):
    flip(b_in, b_ref)
    grad_columns(where, a_ref, b_ref, ka_ref, kb_ref, 2, out)


def grad_kernel(ks, where, *refs):
    for k, out in zip(ks, refs[4:]):
        grad_columns(where, *refs[:4], k, out)


def grad_call(ks, where, a, b, ka, kb, dtype=jnp.bfloat16, first=False):
    out = [jax.ShapeDtypeStruct((4, 2, 2, RB, CB), dtype)] * len(ks)
    return pl.pallas_call(
        first_grad_kernel if first else functools.partial(grad_kernel, ks),
        in_specs=[pl.BlockSpec(memory_space=pltpu.SMEM)] + vmem(4),
        out_specs=vmem(len(ks) + first),
        out_shape=[jax.ShapeDtypeStruct((D // 2, T), jnp.bfloat16)] * first + out,
        cost_estimate=pl.CostEstimate(flops=T * D * KH // 2 * len(ks), bytes_accessed=6 << 20, transcendentals=0),
        compiler_params=pltpu.CompilerParams(vmem_limit_bytes=8 << 20),
        name="grad",
    )(where, a, b, ka, kb)


def add_up(refs):
    total = refs[0][...].astype(jnp.float32)
    for ref in refs[1:]:
        total += ref[...].astype(jnp.float32)
    return total


def first_sum_kernel(*refs):
    for j in range(4):
        refs[4 + j][...] = add_up([ref.at[j] for ref in refs[:4]]).astype(refs[4 + j].dtype)


def first_sum(parts):
    return pl.pallas_call(
        first_sum_kernel,
        in_specs=vmem(4),
        out_specs=vmem(4),
        out_shape=[jax.ShapeDtypeStruct((2, 2, RB, CB), kind) for kind in (jnp.float32,) + (jnp.bfloat16,) * 3],
        cost_estimate=pl.CostEstimate(flops=64 * RB * CB, bytes_accessed=6 << 20, transcendentals=0),
        compiler_params=pltpu.CompilerParams(vmem_limit_bytes=8 << 20),
        name="first_sum",
    )(*parts)


def second_sum_kernel(where, *refs):
    zh = unpack(where)[1]
    for out, h in ((refs[4], zh), (refs[5], 1 - zh)):
        out[...] = add_up([ref.at[h] for ref in refs[:4]]).astype(jnp.bfloat16)


def second_sum(where, parts):
    return pl.pallas_call(
        second_sum_kernel,
        in_specs=[pl.BlockSpec(memory_space=pltpu.SMEM)] + vmem(4),
        out_specs=vmem(2),
        out_shape=[jax.ShapeDtypeStruct((2, RB, CB), jnp.bfloat16)] * 2,
        cost_estimate=pl.CostEstimate(flops=16 * RB * CB, bytes_accessed=2 << 20, transcendentals=0),
        compiler_params=pltpu.CompilerParams(vmem_limit_bytes=4 << 20),
        name="second_sum",
    )(where, *parts)


def total_kernel(own, near, across_z, far, out):
    near_sum = own[...].astype(jnp.float32) + near[...].astype(jnp.float32)
    far_sum = across_z[...].astype(jnp.float32) + far[...].astype(jnp.float32)
    out[...] = (near_sum + far_sum).astype(jnp.bfloat16)


def total_call(*parts):
    return pl.pallas_call(
        total_kernel,
        in_specs=vmem(4),
        out_specs=vmem(1)[0],
        out_shape=jax.ShapeDtypeStruct((2, RB, CB), jnp.bfloat16),
        cost_estimate=pl.CostEstimate(flops=8 * RB * CB, bytes_accessed=1 << 20, transcendentals=0),
        compiler_params=pltpu.CompilerParams(vmem_limit_bytes=4 << 20),
        name="total",
    )(*parts)


def join_kernel(*refs):
    for k, ref in zip(RING, refs[:4]):
        refs[4][k] = ref[...]


def join_call(parts):
    return pl.pallas_call(
        join_kernel,
        in_specs=vmem(4),
        out_specs=vmem(1)[0],
        out_shape=jax.ShapeDtypeStruct((4, 2, RB, CB), jnp.bfloat16),
        cost_estimate=pl.CostEstimate(flops=0, bytes_accessed=1 << 20, transcendentals=0),
        compiler_params=pltpu.CompilerParams(vmem_limit_bytes=4 << 20),
        name="join",
    )(*parts)


SCALE = bias_first * bias_first / bias_second


def old_kernel(me_ref, ve_ref, mc_ref, vc_ref, m_ref, w_ref, hold):
    hold[...] = jnp.zeros_like(hold)
    for part in range(ROWS // 128):
        rows = slice(part * 128, (part + 1) * 128)
        hold[0:4, :] = jnp.exp2(me_ref[:, rows].astype(jnp.float32)) * (0.9 / 127.0)
        hold[4:8, :] = jnp.exp2(ve_ref[:, rows].astype(jnp.float32)) * (0.999 * SCALE / 255.0)
        unit = hold[...].T
        for cb in range(4):
            cols = slice(cb * CB, (cb + 1) * CB)
            m_ref[rows, cols] = mc_ref[rows, cols].astype(jnp.float32) * unit[:, cb:cb + 1]
            w_ref[rows, cols] = vc_ref[rows, cols].astype(jnp.float32) * unit[:, 4 + cb:5 + cb]


def old_call(m_exp, v_exp, m_code, v_code):
    return pl.pallas_call(
        old_kernel,
        in_specs=vmem(4),
        out_specs=vmem(2),
        out_shape=[jax.ShapeDtypeStruct((ROWS, KH), jnp.float32)] * 2,
        scratch_shapes=[pltpu.VMEM((128, 128), jnp.float32)],
        cost_estimate=pl.CostEstimate(flops=4 * ROWS * KH, bytes_accessed=14 << 20, transcendentals=8 * ROWS),
        compiler_params=pltpu.CompilerParams(vmem_limit_bytes=12 << 20),
        name="old",
    )(m_exp.T, v_exp.T, m_code, v_code)


def adam_rows(other, half, read, m_old, w_old, step_ref, mr_ref, vr_ref, keep_scale):
    lane = lax.broadcasted_iota(jnp.int32, (RB, 128), 1)
    for b in range(2):
        rows = slice(b * RB, (b + 1) * RB)
        back = lax.rem(other + 4 - half, 4)
        g = read(back, b).astype(jnp.float32)
        m = m_old[rows, :] + 0.1 * g
        w = w_old[rows, :] + (0.001 * SCALE) * (g * g)
        step_ref[rows, :] = m / (w * lax.rsqrt(w) + 1e-08 * bias_first)
        ms = jnp.max(jnp.abs(m), axis=1, keepdims=True)
        vs = jnp.max(w, axis=1, keepdims=True) * (1.0 / SCALE)
        keep_scale(b, lane, ms, vs)
        mr_ref[rows, :] = (m * (1.0 / (ms + 1e-06))).astype(jnp.bfloat16)
        vr_ref[rows, :] = (w * ((1.0 / SCALE) / (vs + 1e-06))).astype(jnp.bfloat16)


def adam_own_kernel(where, g_ref, m_old, w_old, step_ref, mr_ref, vr_ref, scale_ref):
    _, _, p, other = unpack(where)

    def keep_scale(b, lane, ms, vs):
        scale_ref[b * RB:(b + 1) * RB, :] = jnp.where(lane == p, ms, jnp.where(lane == 4 + p, vs, 0.0))

    adam_rows(
        other, pl.program_id(0), lambda back, zl: g_ref[back, zl],
        m_old, w_old, step_ref, mr_ref, vr_ref, keep_scale,
    )


WIDE = [
    jax.ShapeDtypeStruct((ROWS, KH), jnp.float32),
    jax.ShapeDtypeStruct((ROWS, KH), jnp.bfloat16),
    jax.ShapeDtypeStruct((ROWS, KH), jnp.bfloat16),
]


def adam_own(where, g, old):
    wide = pl.BlockSpec((2 * RB, CB), lambda i, where: (i, (where[0] // 4) % 4))
    thin = pl.BlockSpec((2 * RB, 128), lambda i, where: (i, 0))
    return pl.pallas_call(
        adam_own_kernel,
        grid_spec=pltpu.PrefetchScalarGridSpec(
            num_scalar_prefetch=1,
            grid=(4,),
            in_specs=[pl.BlockSpec((4, 2, RB, CB), lambda i, where: (0, 0, 0, 0)), wide, wide],
            out_specs=[wide, wide, wide, thin],
        ),
        out_shape=WIDE + [jax.ShapeDtypeStruct((ROWS, 128), jnp.float32)],
        cost_estimate=pl.CostEstimate(flops=5 * ROWS * KH, bytes_accessed=4 << 20, transcendentals=ROWS * KH // 2),
        compiler_params=pltpu.CompilerParams(vmem_limit_bytes=10 << 20),
        name="adam_own",
    )(where, g, *old)


def place_of(ks, i, pos):
    k = ks[0]
    for n in range(1, len(ks)):
        k = jnp.where(i < 4 * n, k, ks[n])
    return lax.rem(pos + 4 - k, 4)


def adam_more_kernel(ks, last, where, *refs):
    n = len(ks)
    gs, (m_old, w_old, s0) = refs[:n], refs[n:n + 3]
    step_ref, mr_ref, vr_ref = refs[n + 6:n + 9]
    scales = refs[-1]
    _, _, pos, other = unpack(where)
    i = pl.program_id(0)
    p, half = place_of(ks, i, pos), lax.rem(i, 4)

    @pl.when(i == 0)
    def _():
        scales[...] = s0[...]

    def keep_scale(b, lane, ms, vs):
        rows = pl.ds(pl.multiple_of(half * (2 * RB) + b * RB, 8), RB)
        scales[rows, :] = jnp.where(lane == p, ms, jnp.where(lane == 4 + p, vs, scales[rows, :]))

    def read(back, zl):
        g = gs[0][back, zl]
        for k in range(1, n):
            g = jnp.where(i < 4 * k, g, gs[k][back, zl])
        return g

    adam_rows(other, half, read, m_old, w_old, step_ref, mr_ref, vr_ref, keep_scale)

    if last:
        @pl.when(i == 4 * n - 1)
        def _():
            for part in range(ROWS // 128):
                cols = slice(part * 128, (part + 1) * 128)
                turned = scales[cols, :].T
                refs[n + 9][:, cols] = turned[0:4, :]
                refs[n + 10][:, cols] = turned[4:8, :]


def adam_more(ks, last, where, g, old, s0, done):
    n = len(ks)
    wide = pl.BlockSpec((2 * RB, CB), lambda i, where: (lax.rem(i, 4), place_of(ks, i, (where[0] // 4) % 4)))
    flat = pl.BlockSpec((4, ROWS), lambda i, where: (0, 0))
    tall = pl.BlockSpec((ROWS, 128), lambda i, where: (0, 0))
    whole = pl.BlockSpec((4, 2, RB, CB), lambda i, where: (0, 0, 0, 0))
    scale_shapes = [jax.ShapeDtypeStruct((4, ROWS), jnp.float32)] * 2 if last else [jax.ShapeDtypeStruct((ROWS, 128), jnp.float32)]
    return pl.pallas_call(
        functools.partial(adam_more_kernel, ks, last),
        grid_spec=pltpu.PrefetchScalarGridSpec(
            num_scalar_prefetch=1,
            grid=(4 * n,),
            in_specs=[whole] * n + [wide, wide, tall] + [pl.BlockSpec(memory_space=pl.ANY)] * 3,
            out_specs=[wide, wide, wide] + ([flat, flat] if last else [tall]),
            scratch_shapes=[pltpu.VMEM((ROWS, 128), jnp.float32)] * last,
        ),
        out_shape=WIDE + scale_shapes,
        input_output_aliases={n + 4: 0, n + 5: 1, n + 6: 2},
        cost_estimate=pl.CostEstimate(flops=5 * n * ROWS * KH, bytes_accessed=n * (4 << 20), transcendentals=n * ROWS * KH // 2),
        compiler_params=pltpu.CompilerParams(vmem_limit_bytes=12 << 20),
        name="adam_more",
    )(where, *g, *old, s0, *done)


def dot(a, b):
    return jnp.dot(a, b, preferred_element_type=jnp.float32)


def dot_t(a, b):
    return lax.dot_general(a, b, (((1,), (1,)), ((), ())), preferred_element_type=jnp.float32)


def shard_cols(shard):
    return pl.ds(pl.multiple_of(shard * ROWS, 128), ROWS)


def scale_by_gain(value, gain, shard):
    parts = []
    for part in range(ROWS // 128):
        row = gain[pl.ds(shard * (ROWS // 128) + part, 1), :]
        parts.append(value[:, part * 128:(part + 1) * 128] * row)
    return jnp.concatenate(parts, axis=1)


def half(zh, c, mine, theirs, x, kg, gain, weights, scaled):
    total = dot(mine[:, shard_cols(zh)], weights[0][...]) + dot(theirs[:, shard_cols(zh)], weights[1][...])
    inner = jnp.zeros((T, 1), jnp.float32)
    for k, shard in enumerate((2 * zh + c, 2 * zh + 1 - c)):
        value = scale_by_gain(dot_t(kg[...], weights[k][...]), gain, shard)
        scaled[:, k * ROWS:(k + 1) * ROWS] = value
        inner += jnp.sum(value * x[:, shard_cols(shard)].astype(jnp.float32), axis=1, keepdims=True)
    return total, inner


def near_kernel(where, mine, theirs, x, kg, gain, own, other, keys, inner, scaled):
    c, zh, _, _ = unpack(where)
    keys[...], inner[...] = half(zh, c, mine, theirs, x, kg, gain, (own, other), scaled)


def near_call(where, mine, theirs, tokens, key_grad, gain, own, other):
    return pl.pallas_call(
        near_kernel,
        in_specs=[pl.BlockSpec(memory_space=pltpu.SMEM)] + vmem(7),
        out_specs=vmem(3),
        out_shape=[
            jax.ShapeDtypeStruct((T, KH), jnp.float32),
            jax.ShapeDtypeStruct((T, 1), jnp.float32),
            jax.ShapeDtypeStruct((T, D // 2), jnp.float32),
        ],
        cost_estimate=pl.CostEstimate(flops=2 * T * D * KH, bytes_accessed=18 << 20, transcendentals=0),
        compiler_params=pltpu.CompilerParams(vmem_limit_bytes=12 << 20),
        name="near",
    )(where, mine, theirs, tokens, key_grad, gain, own, other)


def keys_kernel(where, mine, theirs, near, far, far_other, out):
    there = shard_cols(1 - unpack(where)[1])
    total = near[...] + dot(mine[:, there], far[...]) + dot(theirs[:, there], far_other[...])
    out[...] = total.astype(jnp.bfloat16)


def keys_call(where, mine, theirs, near, far, far_other):
    return pl.pallas_call(
        keys_kernel,
        in_specs=[pl.BlockSpec(memory_space=pltpu.SMEM)] + vmem(5),
        out_specs=vmem(1)[0],
        out_shape=jax.ShapeDtypeStruct((T, KH), jnp.bfloat16),
        cost_estimate=pl.CostEstimate(flops=T * D * KH, bytes_accessed=10 << 20, transcendentals=0),
        compiler_params=pltpu.CompilerParams(vmem_limit_bytes=6 << 20),
        name="keys",
    )(where, mine, theirs, near, far, far_other)


def back_kernel(where, x, kg, inv_ref, gain, inner_ref, scaled, far, far_other, out, hold):
    c, zh, _, _ = unpack(where)
    inner = inner_ref[...]
    shards = (2 * (1 - zh) + c, 2 * (1 - zh) + 1 - c)
    for k, (shard, weight) in enumerate(zip(shards, (far, far_other))):
        value = scale_by_gain(dot_t(kg[...], weight[...]), gain, shard)
        hold[:, k * ROWS:(k + 1) * ROWS] = value
        inner += jnp.sum(value * x[:, shard_cols(shard)].astype(jnp.float32), axis=1, keepdims=True)
    inv = inv_ref[...]
    pull = inv * inv * inv * (inner * (1.0 / D))
    for source, shards in ((scaled, (2 * zh + c, 2 * zh + 1 - c)), (hold, shards)):
        for k, shard in enumerate(shards):
            xf = x[:, shard_cols(shard)].astype(jnp.float32)
            value = inv * source[:, k * ROWS:(k + 1) * ROWS] - xf * pull
            out[:, shard_cols(shard)] = value.astype(jnp.bfloat16)


def back_call(where, tokens, key_grad, inv, gain, inner, scaled, far, far_other):
    return pl.pallas_call(
        back_kernel,
        in_specs=[pl.BlockSpec(memory_space=pltpu.SMEM)] + vmem(8),
        out_specs=vmem(1)[0],
        out_shape=jax.ShapeDtypeStruct((T, D), jnp.bfloat16),
        scratch_shapes=[pltpu.VMEM((T, D // 2), jnp.float32)],
        cost_estimate=pl.CostEstimate(flops=T * D * KH, bytes_accessed=16 << 20, transcendentals=0),
        compiler_params=pltpu.CompilerParams(vmem_limit_bytes=14 << 20),
        name="back",
    )(where, tokens, key_grad, inv, gain, inner, scaled, far, far_other)


def device_step(tokens, gain, key_grad, weight, m_code, m_exp, v_code, v_exp):
    zh, c = lax.axis_index("zh"), lax.axis_index("c")
    y, x = lax.axis_index("y"), lax.axis_index("x")
    pos = jnp.where(c == 0, x, y)
    pos_other = jnp.where(c == 0, y, x)
    where = (c + 2 * zh + 4 * pos + 16 * pos_other).astype(jnp.int32).reshape(1)

    gain = gain.reshape(D // 128, 128)

    far = send(weight, across)
    kg_other = send(key_grad, partner)
    w_other = send(weight, partner)

    theirs, inv, tokens, gain = norm_call(where, tokens, gain)
    received = send(theirs, partner)
    mine, mine_t = mine_call(where, tokens, inv, gain)
    received_t, part2 = grad_call((2,), where, mine_t, received, key_grad, kg_other, first=True)
    part2 = send(part2, around(2))
    part1, part3 = grad_call((1, 3), where, mine_t, received_t, key_grad, kg_other)
    part1, part3 = send(part1, around(1)), send(part3, around(3))
    part0, = grad_call((0,), where, mine_t, received_t, key_grad, kg_other, dtype=jnp.float32)
    parts = [part0, part1, part3, part2]
    near_keys, inner, scaled = near_call(where, mine, theirs, tokens, key_grad, gain, weight, w_other)
    old = old_call(m_exp, v_exp, m_code, v_code)
    parts = list(first_sum(parts))
    far_other = send(far, partner)
    parts = [parts[0]] + [send(parts[k], around(k, True)) for k in RING[1:]]
    keys = keys_call(where, mine, theirs, near_keys, far, far_other)
    keep, give = second_sum(where, parts)
    near = send(keep, zl_partner)
    across_z = send(give, across)
    opposite_z = send(give, opposite)
    total = total_call(keep, near, across_z, opposite_z)

    total = join_call([total] + send_ring(total, True))
    got = send_ring(total, False)
    *done, scales = adam_own(where, total, old)
    token_grad = back_call(where, tokens, key_grad, inv, gain, inner, scaled, far, far_other)
    outs = adam_more(RING[1:], True, where, got, old, scales, done)
    step, m_rel, v_rel, m_scale, v_scale = outs
    return keys, token_grad, step, m_rel, m_scale.T, v_rel, v_scale.T


def solution(mesh):
    inner = Mesh(mesh.devices.reshape(2, 2, 4, 4, 2), AXES)
    tok = P(AXES, None)
    row = P(("zh", "c"), None)

    return jax.shard_map(
        device_step,
        mesh=inner,
        in_specs=(tok, P(None), tok, row, row, row, row, row),
        out_specs=(tok, tok, row, row, row, row, row),
        check_vma=False,
    )
```
